768 devices in a mesh: lat: 48 (over x, z), lev: 16 (over y, core).
Axes of the slice: x: 4, y: 8, z: 12, core: 2. Of those that a mesh axis runs over, the one named last changes fastest.
Arguments:
- fields: float32 [4, 128, 192, 2048], P(None, 'lev', 'lat'), may hold values from -6 to 6
- courant_lon: float32 [128, 192, 2048], P('lev', 'lat'), may hold values from -0.45 to 0.45
- courant_lat: float32 [128, 192, 2048], P('lev', 'lat'), may hold values from -0.45 to 0.45
- displacement: float32 [128, 192, 2048], P('lev', 'lat'), may hold values from 0 to 0.6
- own_slot: int32 [16, 48, 2], P('lev', 'lat'), may hold values from 0 to 4, as said below
- lent_slot: int32 [16, 48, 2], P('lev', 'lat'), may hold values from 0 to 4, as said below
- w_first: bfloat16 [512, 768], replicated, may hold values from -0.25 to 0.25
- bias_first: float32 [768], replicated, may hold values from -3 to 3
- w_second: bfloat16 [768, 640], replicated, may hold values from -0.21875 to 0.21875
- bias_second: float32 [640], replicated, may hold values from -3 to 3
- w_third: bfloat16 [640, 512], replicated, may hold values from -0.25 to 0.25
- bias_third: float32 [512], replicated, may hold values from -3 to 3
Outputs:
- columns_out: float32 [512, 192, 2048], P(None, 'lat', 'lev')
The draws below stay inside these ranges and needn't reach their ends.
Inputs may be any that keep to these rules, and one draw needn't show every extreme that they name: own_slot[g, i, s] is a block of band i and group g (0 to 3) handled in work slot s of that band, or 4 when the slot takes no own block; own blocks fill the first slots. lent_slot[g, i, s] is a block of band i and group g handled in work slot s of band (i + 24) mod 48 of group g, or 4; that slot then holds no own block there; no block appears twice in the two lists of its band and group.
All inputs are finite; a program needn't handle non-finite values.
Results may differ from the reference program's by a relative error of at most 0.002.
Values may be sent and summed in bfloat16 or wider, within the bound.
A program may use at most 32 MiB of HBM per device.

```python
import jax
import jax.numpy as jnp
from jax import lax

F = 4
LEV = 128
H1 = 768
H2 = 640
BLOCK = 128
LAT_DEV = 4
LON_DEV = 128
IN = 512
BANDS = 48
GROUPS = 16
LAT = 192
LON = 2048
BLK_DEV = 4
WORK = 2


def slot_plan(key):
    base_key = jax.random.fold_in(key, 11)
    key_list = jax.random.split(base_key, 4)
    half_bands = BANDS // 2
    first_count = jax.random.randint(key_list[0], (GROUPS, half_bands), 0, BLK_DEV + 1)
    second_count = jax.random.randint(key_list[1], (GROUPS, half_bands), 0, BLK_DEV + 1) % (BLK_DEV - first_count + 1)
    flip_pair = jax.random.randint(key_list[2], (GROUPS, half_bands), 0, 2)
    live_count = jnp.concatenate([jnp.where(flip_pair == 1, second_count, first_count), jnp.where(flip_pair == 1, first_count, second_count)], axis=1)
    rank_scores = jax.random.randint(key_list[3], (GROUPS, BANDS, BLK_DEV), 0, 1 << 20) * BLK_DEV + jnp.arange(BLK_DEV, dtype=jnp.int32)
    block_order = jnp.argsort(rank_scores, axis=-1).astype(jnp.int32)
    slot_index = jnp.arange(WORK, dtype=jnp.int32)
    kept_count = jnp.minimum(live_count, WORK)
    extra_count = jnp.maximum(live_count - WORK, 0)
    own_list = jnp.where(slot_index < kept_count[..., None], block_order[..., :WORK], BLK_DEV)
    partner_count = jnp.roll(live_count, -half_bands, axis=1)
    slot_offset = slot_index - jnp.minimum(partner_count, WORK)[..., None]
    lent_valid = (slot_offset >= 0) & (slot_offset < extra_count[..., None])
    pick_index = jnp.clip(WORK + slot_offset, 0, BLK_DEV - 1).astype(jnp.int32)
    lent_block = jnp.take_along_axis(block_order, pick_index, axis=-1)
    lent_list = jnp.where(lent_valid, lent_block, BLK_DEV)
    return (own_list.astype(jnp.int32), lent_list.astype(jnp.int32))


def draw_own_slot(key, part):
    return slot_plan(key)[0]


def draw_lent_slot(key, part):
    return slot_plan(key)[1]


def block_scale(own_key, extent, shards, least, largest):
    level = 1.0
    for position, parts in shards:
        steps = jax.random.uniform(jax.random.fold_in(jax.random.fold_in(own_key, 6), position), (parts,), jnp.float32, least / len(shards), largest / len(shards))
        level = level * jnp.repeat(jnp.exp(steps), extent[position] // parts).reshape((-1,) + (1,) * (len(extent) - 1 - position))
    return level


def scatter_about(stream_key, shape, spread, most, shards=(), kind=jnp.bfloat16):
    array = jax.random.normal(stream_key, shape, jnp.float32) * spread
    if len(shards) > 0:
        array = block_scale(stream_key, shape, shards, -0.22, 0.18) * array
    return jnp.clip(array, min=-most, max=most).astype(kind)


def setup_inputs(seed: int = 0) -> dict:
    keys = jax.random.split(jax.random.key(seed), 13)
    return {
        "fields": scatter_about(keys[0], (F, LEV, LAT, LON), 1.0, 6.0, ((1, 16), (2, 48)), jnp.float32),
        "courant_lon": jnp.clip(jax.random.uniform(keys[1], (LEV, LAT, LON), jnp.float32, -0.45, 0.45) * block_scale(keys[1], (LEV, LAT, LON), ((0, 16), (1, 48)), -0.4, 0.0), -0.45, 0.45),
        "courant_lat": jnp.clip(jax.random.uniform(keys[2], (LEV, LAT, LON), jnp.float32, -0.45, 0.45) * block_scale(keys[2], (LEV, LAT, LON), ((0, 16), (1, 48)), -0.4, 0.0), -0.45, 0.45),
        "displacement": jnp.clip(0.6 * jax.random.uniform(keys[3], (LEV, LAT, LON), jnp.float32) ** block_scale(keys[3], (LEV, LAT, LON), ((0, 16), (1, 48)), -0.2, 0.2), 0.0, 0.6),
        "own_slot": draw_own_slot(jax.random.fold_in(keys[12], 71), 0),
        "lent_slot": draw_lent_slot(jax.random.fold_in(keys[12], 71), 0),
        "w_first": scatter_about(keys[6], (IN, H1), IN ** -0.5, 0.25),
        "bias_first": scatter_about(keys[7], (H1,), 0.5, 3.0, (), jnp.float32),
        "w_second": scatter_about(keys[8], (H1, H2), H1 ** -0.5, 0.21875),
        "bias_second": scatter_about(keys[9], (H2,), 0.5, 3.0, (), jnp.float32),
        "w_third": scatter_about(keys[10], (H2, IN), H2 ** -0.5, 0.25),
        "bias_third": scatter_about(keys[11], (IN,), 0.5, 3.0, (), jnp.float32),
    }


def upwind(fields, western, eastern, northern, southern, along_lon, along_lat):
    result = fields - jnp.maximum(along_lon, 0.0) * (fields - western)
    result = result - jnp.minimum(along_lon, 0.0) * (eastern - fields)
    result = result - jnp.maximum(along_lat, 0.0) * (fields - northern)
    return result - jnp.minimum(along_lat, 0.0) * (southern - fields)


def network(rows, w_first, bias_first, w_second, bias_second, w_third, bias_third):
    hidden = jnp.dot(rows, w_first, preferred_element_type=jnp.float32) + bias_first
    hidden = jax.nn.silu(hidden).astype(jnp.bfloat16)
    hidden = jnp.dot(hidden, w_second, preferred_element_type=jnp.float32) + bias_second
    hidden = jax.nn.silu(hidden).astype(jnp.bfloat16)
    return (jnp.dot(hidden, w_third, preferred_element_type=jnp.float32) + bias_third).astype(jnp.bfloat16)


def reference(fields, courant_lon, courant_lat, displacement, own_slot, lent_slot, w_first, bias_first, w_second, bias_second, w_third, bias_third):
    padded = jnp.pad(fields, ((0, 0), (0, 0), (1, 1), (0, 0)))
    advected = upwind(fields, jnp.roll(fields, 1, axis=3), jnp.roll(fields, -1, axis=3), padded[:, :, :-2, :], padded[:, :, 2:, :], courant_lon[None], courant_lat[None])
    depth = lax.broadcasted_iota(jnp.int32, (1, LEV, 1, 1), 1)
    flux = jnp.where(depth < LEV - 1, displacement[None] * advected, 0.0)
    above = jnp.concatenate([jnp.zeros_like(flux[:, :1]), flux[:, :-1]], axis=1)
    remapped = advected - flux + above
    width = F * LEV
    columns = jnp.transpose(remapped, (2, 3, 0, 1)).reshape(LAT, LON, width)
    blocks = columns.reshape(BANDS, LAT_DEV, GROUPS, LON_DEV, width).transpose(2, 0, 1, 3, 4).reshape(GROUPS, BANDS, BLK_DEV, BLOCK, width)
    inputs = blocks.astype(jnp.bfloat16)
    own_safe = jnp.minimum(own_slot, BLK_DEV - 1).astype(jnp.int32)
    lent_safe = jnp.minimum(lent_slot, BLK_DEV - 1).astype(jnp.int32)
    own_rows = jnp.take_along_axis(inputs, own_safe[:, :, :, None, None], axis=2)
    lent_rows = jnp.take_along_axis(inputs, lent_safe[:, :, :, None, None], axis=2)
    lent_rows = jnp.where((lent_slot < BLK_DEV)[:, :, :, None, None], lent_rows, jnp.zeros_like(lent_rows))
    arrived = jnp.roll(lent_rows, -(BANDS // 2), axis=1)
    work_rows = jnp.where((own_slot < BLK_DEV)[:, :, :, None, None], own_rows, arrived)

    def per_group(group_rows):
        flat = network(group_rows.reshape(-1, width), w_first, bias_first, w_second, bias_second, w_third, bias_third)
        return flat.reshape(group_rows.shape)

    tendency = lax.map(per_group, work_rows)
    returned = jnp.roll(tendency, -(BANDS // 2), axis=1)
    block_ids = lax.broadcasted_iota(jnp.int32, (1, 1, BLK_DEV, 1, 1), 2)
    added = jnp.zeros(blocks.shape, jnp.float32)
    for slot_number in range(WORK):
        own_hit = own_slot[:, :, slot_number][:, :, None, None, None] == block_ids
        lent_hit = lent_slot[:, :, slot_number][:, :, None, None, None] == block_ids
        added = added + jnp.where(own_hit, tendency[:, :, slot_number][:, :, None].astype(jnp.float32), 0.0)
        added = added + jnp.where(lent_hit, returned[:, :, slot_number][:, :, None].astype(jnp.float32), 0.0)
    result = blocks + added
    return result.reshape(GROUPS, BANDS, LAT_DEV, LON_DEV, width).transpose(4, 1, 2, 0, 3).reshape(width, LAT, LON)
```

```python
import jax
import jax.numpy as jnp
from jax import lax
from jax.sharding import PartitionSpec as P


def padded_lat(value):
    count, length = lax.axis_size("lat"), value.shape[2]
    up = [(i, i + 1) for i in range(count - 1)]
    down = [(j, i) for i, j in up]
    ends = value.astype(jnp.bfloat16)
    last = lax.slice_in_dim(ends, length - 1, length, axis=2)
    first = lax.slice_in_dim(ends, 0, 1, axis=2)
    before = lax.ppermute(last, "lat", up).astype(value.dtype)
    after = lax.ppermute(first, "lat", down).astype(value.dtype)
    return jnp.concatenate([before, value, after], axis=2)


def upwind(fields, western, eastern, northern, southern, along_lon, along_lat):
    result = fields - jnp.maximum(along_lon, 0.0) * (fields - western)
    result = result - jnp.minimum(along_lon, 0.0) * (eastern - fields)
    result = result - jnp.maximum(along_lat, 0.0) * (fields - northern)
    return result - jnp.minimum(along_lat, 0.0) * (southern - fields)


def left_product(weight, rows):
    return lax.dot_general(
        weight, rows, (((0,), (0,)), ((), ())), preferred_element_type=jnp.float32
    )


def network(rows, w_first, bias_first, w_second, bias_second, w_third, bias_third):
    hidden = left_product(w_first, rows) + bias_first[:, None]
    hidden = jax.nn.silu(hidden).astype(jnp.bfloat16)
    hidden = left_product(w_second, hidden) + bias_second[:, None]
    hidden = jax.nn.silu(hidden).astype(jnp.bfloat16)
    return left_product(w_third, hidden) + bias_third[:, None]


def body(
    fields,
    courant_lon,
    courant_lat,
    displacement,
    own_slot,
    lent_slot,
    w_first,
    bias_first,
    w_second,
    bias_second,
    w_third,
    bias_third,
):
    field_count, level_part, band_rows, lon_total = fields.shape
    group_count = lax.axis_size("lev")
    lon_part = lon_total // group_count
    padded = padded_lat(fields)
    advected = upwind(
        fields,
        jnp.roll(fields, 1, axis=3),
        jnp.roll(fields, -1, axis=3),
        padded[:, :, :-2, :],
        padded[:, :, 2:, :],
        courant_lon[None],
        courant_lat[None],
    )
    flux = displacement[None] * advected
    lowest = flux[:, level_part - 1 :].astype(jnp.bfloat16)
    steps = [(i, i + 1) for i in range(group_count - 1)]
    entering = lax.ppermute(lowest, "lev", steps).astype(jnp.float32)
    depth = lax.broadcasted_iota(jnp.int32, (1, level_part, 1, 1), 1)
    bottom = lax.axis_index("lev") * level_part + depth == group_count * level_part - 1
    above = jnp.concatenate([entering, flux[:, : level_part - 1]], axis=1)
    remapped = advected - jnp.where(bottom, 0.0, flux) + above
    split = remapped.astype(jnp.bfloat16).reshape(
        field_count, level_part, band_rows, group_count, lon_part
    )
    moved = lax.all_to_all(split, "lev", split_axis=3, concat_axis=1, tiled=True)
    width = field_count * level_part * group_count
    rows = moved.reshape(width, band_rows * lon_part)
    tendency = network(
        rows, w_first, bias_first, w_second, bias_second, w_third, bias_third
    )
    slots = jnp.concatenate([own_slot.reshape(-1), lent_slot.reshape(-1)])
    block_ids = jnp.arange(band_rows, dtype=jnp.int32)
    active = jnp.any(slots[None, :] == block_ids[:, None], axis=1)
    shape = (width, band_rows, lon_part)
    added = jnp.where(active[None, :, None], tendency.reshape(shape), 0.0)
    return rows.reshape(shape).astype(jnp.float32) + added


def solution(mesh):
    in_specs = (
        P(None, "lev", "lat", None),
        P("lev", "lat", None),
        P("lev", "lat", None),
        P("lev", "lat", None),
        P("lev", "lat", None),
        P("lev", "lat", None),
        P(),
        P(),
        P(),
        P(),
        P(),
        P(),
    )
    out_specs = P(None, "lat", "lev")
    return jax.shard_map(body, mesh=mesh, in_specs=in_specs, out_specs=out_specs, check_vma=False)
```

```python
import jax
import jax.numpy as jnp
from jax import lax
from jax.experimental import pallas as pl
from jax.experimental.pallas import tpu as pltpu
from jax.sharding import PartitionSpec as P

MESH = pl.DeviceIdType.MESH
PAIRS = ((1, 2), (0, 3))


def silu(value):
    return value * (0.5 + 0.5 * jnp.tanh(0.5 * value))


def kernel(
    fields_hbm,
    lon_hbm,
    lat_hbm,
    move_hbm,
    own_hbm,
    lent_hbm,
    w1_hbm,
    b1_hbm,
    w2_hbm,
    b2_hbm,
    w3_hbm,
    b3_hbm,
    out_hbm,
    fb,
    cb,
    part,
    halo_out,
    halo_in,
    flux_out,
    flux_in,
    send,
    recv,
    w1,
    w2,
    w3,
    w1t,
    w2t,
    w3t,
    b1,
    b2,
    b3,
    ob,
    h1,
    h2,
    own_ref,
    lent_ref,
    b1_line,
    b2_line,
    b3_line,
    field_sem,
    wind_sem,
    weight_sem,
    out_sem,
    halo_send_sem,
    halo_recv_sem,
    flux_send_sem,
    flux_recv_sem,
    send_sem,
    recv_sem,
):
    count = lax.axis_size("lev")
    bands = lax.axis_size("lat")
    lev = lax.axis_index("lev")
    lat = lax.axis_index("lat")
    north, south = lax.rem(lat + bands - 1, bands), lax.rem(lat + 1, bands)
    nfield, nrow, nlev, lon = fb.shape

    field_copies = {}
    wind_copies = {}
    for r in (0, 3, 1, 2):
        field_copies[r] = pltpu.make_async_copy(
            fields_hbm.at[:, :, r, :], fb.at[:, r], field_sem.at[r]
        )
        field_copies[r].start()
    for r in (1, 2, 0, 3):
        for i, src in enumerate((lon_hbm, lat_hbm, move_hbm)):
            wind_copies[i, r] = pltpu.make_async_copy(
                src.at[:, r, :], cb.at[i, r], wind_sem.at[i, r]
            )
            wind_copies[i, r].start()
    weight_copies = []
    moves = (
        (w1_hbm, w1),
        (b1_hbm, b1_line),
        (b2_hbm, b2_line),
        (b3_hbm, b3_line),
        (own_hbm, own_ref),
        (lent_hbm, lent_ref),
        (w2_hbm, w2),
        (w3_hbm, w3),
    )
    for i, (src, dst) in enumerate(moves):
        weight_copies.append(pltpu.make_async_copy(src, dst, weight_sem.at[i]))
        weight_copies[i].start()

    barrier = pltpu.get_barrier_semaphore()
    for off in range(1, count):
        pl.semaphore_signal(
            barrier, 1, device_id={"lev": lax.rem(lev + off, count)}, device_id_type=MESH
        )
    for other in (north, south):
        pl.semaphore_signal(barrier, 1, device_id={"lat": other}, device_id_type=MESH)

    sub = lax.broadcasted_iota(jnp.int32, (nlev, lon), 0)

    def advect(r, k):
        lonp = jnp.maximum(cb[0, r], 0.0)
        lonn = jnp.minimum(cb[0, r], 0.0)
        latp = jnp.maximum(cb[1, r], 0.0)
        latn = jnp.minimum(cb[1, r], 0.0)
        move = cb[2, r]
        last = jnp.logical_and(sub == nlev - 1, lev == count - 1)
        move = jnp.where(last, 0.0, move)
        for f in range(nfield):
            x = fb[f, r]
            half = pl.ds((f % 2) * nlev, nlev)
            if r == 0:
                up = halo_in[0, f // 2].astype(jnp.float32)
                up = up[(f % 2) * nlev : (f % 2 + 1) * nlev]
                up = jnp.where(lat == 0, 0.0, up)
            else:
                up = fb[f, r - 1]
            if r == nrow - 1:
                down = halo_in[1, f // 2].astype(jnp.float32)
                down = down[(f % 2) * nlev : (f % 2 + 1) * nlev]
                down = jnp.where(lat == bands - 1, 0.0, down)
            else:
                down = fb[f, r + 1]
            value = x - lonp * (x - pltpu.roll(x, 1, 1))
            value = value - lonn * (pltpu.roll(x, lon - 1, 1) - x)
            value = value - latp * (x - up)
            value = value - latn * (down - x)
            flux = move * value
            turned = pltpu.roll(flux, 1, 0)
            part[f, r] = value - flux + jnp.where(sub == 0, 0.0, turned)
            flux_out[k // 4, (k % 4) * nfield + f : (k % 4) * nfield + f + 1, :] = turned[0:1]

    def flux_copy(p):
        return pltpu.make_async_remote_copy(
            src_ref=flux_out.at[p],
            dst_ref=flux_in.at[p],
            send_sem=flux_send_sem.at[p],
            recv_sem=flux_recv_sem.at[p],
            device_id={"lev": lax.rem(lev + 1, count)},
            device_id_type=MESH,
        )

    def halo_copy(i):
        return pltpu.make_async_remote_copy(
            src_ref=halo_out.at[i],
            dst_ref=halo_in.at[i],
            send_sem=halo_send_sem.at[i],
            recv_sem=halo_recv_sem.at[i],
            device_id={"lat": south if i == 0 else north},
            device_id_type=MESH,
        )

    def block_copy(p, off):
        target = lax.rem(lev + off, count)
        return pltpu.make_async_remote_copy(
            src_ref=send.at[p, target],
            dst_ref=recv.at[p, lev],
            send_sem=send_sem.at[p, off - 1],
            recv_sem=recv_sem.at[p, off - 1],
            device_id={"lev": target},
            device_id_type=MESH,
        )

    def finish(p):
        for i, r in enumerate(PAIRS[p]):
            for pair in range(nfield // 2):
                values = []
                for f in (2 * pair, 2 * pair + 1):
                    enter = flux_in[p, i * nfield + f : i * nfield + f + 1, :]
                    enter = jnp.broadcast_to(enter, (nlev, lon))
                    values.append(part[f, r] + jnp.where(sub == 0, enter, 0.0))
                both = jnp.concatenate(values, axis=0).astype(jnp.bfloat16)
                row = i * nfield * nlev + pair * 2 * nlev
                for g in range(16):
                    send[p, g, row : row + 2 * nlev, :] = both[:, g * 128 : (g + 1) * 128]
        for off in ORDER:
            block_copy(p, off).start()

    field_copies[0].wait()
    field_copies[3].wait()
    for i, r in ((0, 3), (1, 0)):
        for pair in range(nfield // 2):
            both = jnp.concatenate([fb[2 * pair, r], fb[2 * pair + 1, r]], axis=0)
            halo_out[i, pair] = both.astype(jnp.bfloat16)
    field_copies[1].wait()
    field_copies[2].wait()
    for k, r in enumerate(PAIRS[0]):
        for i in range(3):
            wind_copies[i, r].wait()
        advect(r, k)

    pl.semaphore_wait(barrier, count + 1)
    flux_copy(0).start()
    for i in range(2):
        halo_copy(i).start()

    for copy in weight_copies:
        copy.wait()
    w1t[...] = w1[...].T

    flux_copy(0).wait_recv()
    finish(0)

    for r in PAIRS[1]:
        for i in range(3):
            wind_copies[i, r].wait()
    for i in range(2):
        halo_copy(i).wait_recv()
    for k, r in enumerate(PAIRS[1]):
        advect(r, 4 + k)
    flux_copy(1).start()
    w2t[...] = w2[...].T
    flux_copy(1).wait_recv()
    finish(1)

    w3t[...] = w3[...].T
    for src, dst in ((b1_line, b1), (b2_line, b2), (b3_line, b3)):
        for i in range(dst.shape[0] // 128):
            line = jnp.broadcast_to(src[i * 128 : (i + 1) * 128][None], (128, 128))
            dst[i * 128 : (i + 1) * 128, :] = line.T

    def unpack(p, block, source):
        for i, r in enumerate(PAIRS[p]):
            for f in range(nfield):
                row = i * nfield * nlev + f * nlev
                start = pl.multiple_of(f * nlev * count + source * nlev, 8)
                ob[r, pl.ds(start, nlev), :] = block[row : row + nlev]

    def twice(value):
        return jnp.concatenate([value, value], axis=1)

    def physics(p):
        ra, rb = PAIRS[p]
        x = jnp.concatenate([ob[ra], ob[rb]], axis=1).astype(jnp.bfloat16)
        for start in range(0, 768, 256):
            rows = slice(start, start + 256)
            v = jnp.dot(w1t[rows], x, preferred_element_type=jnp.float32)
            h1[rows] = silu(v + twice(b1[rows])).astype(jnp.bfloat16)
        x = h1[...]
        for start in range(0, 640, 128):
            rows = slice(start, start + 128)
            v = jnp.dot(w2t[rows], x, preferred_element_type=jnp.float32)
            h2[rows] = silu(v + twice(b2[rows])).astype(jnp.bfloat16)
        x = h2[...]
        active = []
        for r in (ra, rb):
            hit = own_ref[0, 0, 0] == r
            for other in (own_ref[0, 0, 1], lent_ref[0, 0, 0], lent_ref[0, 0, 1]):
                hit = jnp.logical_or(hit, other == r)
            active.append(hit)
        for start in range(0, 512, 256):
            rows = slice(start, start + 256)
            v = jnp.dot(w3t[rows], x, preferred_element_type=jnp.float32)
            v = (v + twice(b3[rows])).astype(jnp.bfloat16).astype(jnp.float32)
            for i, r in enumerate((ra, rb)):
                ob[r, rows] = ob[r, rows] + jnp.where(
                    active[i], v[:, i * 128 : (i + 1) * 128], 0.0
                )
        for r in (ra, rb):
            out_copy(r).start()

    def out_copy(r):
        return pltpu.make_async_copy(ob.at[r], out_hbm.at[:, r, :], out_sem.at[r])

    for p in range(2):
        unpack(p, send[p, lev].astype(jnp.float32), lev)
        for off in ORDER:
            block_copy(p, off).wait_recv()
            source = lax.rem(lev + count - off, count)
            unpack(p, recv[p, source].astype(jnp.float32), source)
        physics(p)

    for p in range(2):
        flux_copy(p).wait_send()
        halo_copy(p).wait_send()
        for off in ORDER:
            block_copy(p, off).wait_send()
    for r in range(nrow):
        out_copy(r).wait()


ORDER = (8, 7, 9, 6, 10, 5, 11, 4, 12, 3, 13, 2, 14, 1, 15)


def in_hbm(value):
    return pltpu.with_memory_space_constraint(value, pltpu.HBM)


def body(
    fields,
    courant_lon,
    courant_lat,
    displacement,
    own_slot,
    lent_slot,
    w_first,
    bias_first,
    w_second,
    bias_second,
    w_third,
    bias_third,
):
    nfield, nlev, nrow, lon = fields.shape
    count = lax.axis_size("lev")
    width = nfield * nlev * count
    part = lon // count
    hidden = (w_first.shape[1], w_second.shape[1])
    f32, bf16 = jnp.float32, jnp.bfloat16
    hbm = pl.BlockSpec(memory_space=pltpu.HBM)
    dma = pltpu.SemaphoreType.DMA
    return pl.pallas_call(
        kernel,
        name="tracer",
        out_shape=jax.ShapeDtypeStruct((width, nrow, part), f32),
        in_specs=[hbm] * 12,
        out_specs=pl.BlockSpec(memory_space=pl.ANY),
        scratch_shapes=[
            pltpu.VMEM((nfield, nrow, nlev, lon), f32),
            pltpu.VMEM((3, nrow, nlev, lon), f32),
            pltpu.VMEM((nfield, nrow, nlev, lon), f32),
            pltpu.VMEM((2, nfield // 2, 2 * nlev, lon), bf16),
            pltpu.VMEM((2, nfield // 2, 2 * nlev, lon), bf16),
            pltpu.VMEM((2, 2 * nfield, lon), f32),
            pltpu.VMEM((2, 2 * nfield, lon), f32),
            pltpu.VMEM((2, count, 2 * nfield * nlev, part), bf16),
            pltpu.VMEM((2, count, 2 * nfield * nlev, part), bf16),
            pltpu.VMEM((width, hidden[0]), bf16),
            pltpu.VMEM((hidden[0], hidden[1]), bf16),
            pltpu.VMEM((hidden[1], width), bf16),
            pltpu.VMEM((hidden[0], width), bf16),
            pltpu.VMEM((hidden[1], hidden[0]), bf16),
            pltpu.VMEM((width, hidden[1]), bf16),
            pltpu.VMEM((hidden[0], 128), f32),
            pltpu.VMEM((hidden[1], 128), f32),
            pltpu.VMEM((width, 128), f32),
            pltpu.VMEM((nrow, width, part), f32),
            pltpu.VMEM((hidden[0], 2 * part), bf16),
            pltpu.VMEM((hidden[1], 2 * part), bf16),
            pltpu.SMEM(own_slot.shape, jnp.int32),
            pltpu.SMEM(lent_slot.shape, jnp.int32),
            pltpu.VMEM(bias_first.shape, f32),
            pltpu.VMEM(bias_second.shape, f32),
            pltpu.VMEM(bias_third.shape, f32),
            dma((nrow,)),
            dma((3, nrow)),
            dma((8,)),
            dma((nrow,)),
            dma((2,)),
            dma((2,)),
            dma((2,)),
            dma((2,)),
            dma((2, count - 1)),
            dma((2, count - 1)),
        ],
        compiler_params=pltpu.CompilerParams(
            collective_id=0, has_side_effects=True, vmem_limit_bytes=48 << 20
        ),
    )(
        in_hbm(fields),
        in_hbm(courant_lon),
        in_hbm(courant_lat),
        in_hbm(displacement),
        in_hbm(own_slot),
        in_hbm(lent_slot),
        in_hbm(w_first),
        in_hbm(bias_first),
        in_hbm(w_second),
        in_hbm(bias_second),
        in_hbm(w_third),
        in_hbm(bias_third),
    )


def solution(mesh):
    in_specs = (
        P(None, "lev", "lat", None),
        P("lev", "lat", None),
        P("lev", "lat", None),
        P("lev", "lat", None),
        P("lev", "lat", None),
        P("lev", "lat", None),
        P(),
        P(),
        P(),
        P(),
        P(),
        P(),
    )
    out_specs = P(None, "lat", "lev")
    return jax.shard_map(body, mesh=mesh, in_specs=in_specs, out_specs=out_specs, check_vma=False)
```

```python
import jax
import jax.numpy as jnp
from jax import lax
from jax.experimental import pallas as pl
from jax.experimental.pallas import tpu as pltpu
from jax.sharding import PartitionSpec as P

MESH = pl.DeviceIdType.MESH
PAIRS = ((1, 2), (0, 3))


def silu(value):
    return value * (0.5 + 0.5 * jnp.tanh(0.5 * value))


def kernel(
    fields_hbm,
    lon_hbm,
    lat_hbm,
    move_hbm,
    own_hbm,
    lent_hbm,
    w1_hbm,
    b1_hbm,
    w2_hbm,
    b2_hbm,
    w3_hbm,
    b3_hbm,
    out,
    fb,
    cb,
    part,
    halo_out,
    halo_in,
    flux_row,
    flux_out,
    flux_in,
    send,
    recv,
    w1,
    w2,
    w3,
    w1t,
    w2t,
    w3t,
    b1,
    b2,
    b3,
    ob,
    x_buf,
    h1,
    h2,
    own_ref,
    lent_ref,
    b1_line,
    b2_line,
    b3_line,
    field_sem,
    wind_sem,
    weight_sem,
    halo_send_sem,
    halo_recv_sem,
    flux_send_sem,
    flux_recv_sem,
    send_sem,
    recv_sem,
):
    count = lax.axis_size("lev")
    bands = lax.axis_size("lat")
    lev = lax.axis_index("lev")
    lat = lax.axis_index("lat")
    north, south = lax.rem(lat + bands - 1, bands), lax.rem(lat + 1, bands)
    nfield, nrow, nlev, lon = fb.shape

    field_copies = {}
    wind_copies = {}
    for r in (0, 3, 1, 2):
        field_copies[r] = pltpu.make_async_copy(
            fields_hbm.at[:, :, r, :], fb.at[:, r], field_sem.at[r]
        )
        field_copies[r].start()
    for r in (1, 2, 0, 3):
        for i, src in enumerate((lon_hbm, lat_hbm, move_hbm)):
            wind_copies[i, r] = pltpu.make_async_copy(
                src.at[:, r, :], cb.at[i, r], wind_sem.at[i, r]
            )
            wind_copies[i, r].start()
    weight_copies = []
    moves = (
        (w1_hbm, w1),
        (b1_hbm, b1_line),
        (b2_hbm, b2_line),
        (b3_hbm, b3_line),
        (own_hbm, own_ref),
        (lent_hbm, lent_ref),
        (w2_hbm, w2),
        (w3_hbm, w3),
    )
    for i, (src, dst) in enumerate(moves):
        weight_copies.append(pltpu.make_async_copy(src, dst, weight_sem.at[i]))

    barrier = pltpu.get_barrier_semaphore()
    for off in range(1, count):
        pl.semaphore_signal(
            barrier, 1, device_id={"lev": lax.rem(lev + off, count)}, device_id_type=MESH
        )
    for other in (north, south):
        pl.semaphore_signal(barrier, 1, device_id={"lat": other}, device_id_type=MESH)

    sub = lax.broadcasted_iota(jnp.int32, (nlev, lon), 0)

    def advect(r, k):
        lonp = jnp.maximum(cb[0, r], 0.0)
        lonn = jnp.minimum(cb[0, r], 0.0)
        latp = jnp.maximum(cb[1, r], 0.0)
        latn = jnp.minimum(cb[1, r], 0.0)
        move = cb[2, r]
        last = jnp.logical_and(sub == nlev - 1, lev == count - 1)
        move = jnp.where(last, 0.0, move)
        for f in range(nfield):
            x = fb[f, r]
            half = pl.ds((f % 2) * nlev, nlev)
            if r == 0:
                up = halo_in[0, f // 2].astype(jnp.float32)
                up = up[(f % 2) * nlev : (f % 2 + 1) * nlev]
                up = jnp.where(lat == 0, 0.0, up)
            else:
                up = fb[f, r - 1]
            if r == nrow - 1:
                down = halo_in[1, f // 2].astype(jnp.float32)
                down = down[(f % 2) * nlev : (f % 2 + 1) * nlev]
                down = jnp.where(lat == bands - 1, 0.0, down)
            else:
                down = fb[f, r + 1]
            value = x - lonp * (x - pltpu.roll(x, 1, 1))
            value = value - lonn * (pltpu.roll(x, lon - 1, 1) - x)
            value = value - latp * (x - up)
            value = value - latn * (down - x)
            flux = move * value
            turned = pltpu.roll(flux, 1, 0)
            part[f, r] = value - flux + jnp.where(sub == 0, 0.0, turned)
            flux_row[k * nfield + f : k * nfield + f + 1, :] = turned[0:1]

    def flux_copy(p, off):
        target = lax.rem(lev + off, count)
        return pltpu.make_async_remote_copy(
            src_ref=flux_out.at[p, target],
            dst_ref=flux_in.at[p, lev],
            send_sem=flux_send_sem.at[p, off - 1],
            recv_sem=flux_recv_sem.at[p, off - 1],
            device_id={"lev": target},
            device_id_type=MESH,
        )

    def halo_copy(i):
        return pltpu.make_async_remote_copy(
            src_ref=halo_out.at[i],
            dst_ref=halo_in.at[i],
            send_sem=halo_send_sem.at[i],
            recv_sem=halo_recv_sem.at[i],
            device_id={"lat": south if i == 0 else north},
            device_id_type=MESH,
        )

    def block_copy(p, off):
        target = lax.rem(lev + off, count)
        return pltpu.make_async_remote_copy(
            src_ref=send.at[p, target],
            dst_ref=recv.at[p, lev],
            send_sem=send_sem.at[p, off - 1],
            recv_sem=recv_sem.at[p, off - 1],
            device_id={"lev": target},
            device_id_type=MESH,
        )

    def finish(p):
        for i, r in enumerate(PAIRS[p]):
            for pair in range(nfield // 2):
                both = jnp.concatenate([part[2 * pair, r], part[2 * pair + 1, r]], axis=0)
                both = both.astype(jnp.bfloat16)
                row = i * nfield * nlev + pair * 2 * nlev
                for g in range(16):
                    send[p, g, row : row + 2 * nlev, :] = both[:, g * 128 : (g + 1) * 128]
        edge = flux_row[...].astype(jnp.bfloat16)
        for g in range(16):
            flux_out[p, g] = edge[:, g * 128 : (g + 1) * 128]
        for off in ORDER:
            flux_copy(p, off).start()
            block_copy(p, off).start()
        recv[p, lev] = send[p, lev]
        flux_in[p, lev] = flux_out[p, lev]

    field_copies[0].wait()
    field_copies[3].wait()
    for i, r in ((0, 3), (1, 0)):
        for pair in range(nfield // 2):
            both = jnp.concatenate([fb[2 * pair, r], fb[2 * pair + 1, r]], axis=0)
            halo_out[i, pair] = both.astype(jnp.bfloat16)
    field_copies[1].wait()
    field_copies[2].wait()
    for k, r in enumerate(PAIRS[0]):
        for i in range(3):
            wind_copies[i, r].wait()
        advect(r, k)
    for copy in weight_copies:
        copy.start()

    pl.semaphore_wait(barrier, count + 1)
    for i in range(2):
        halo_copy(i).start()
    finish(0)

    for r in PAIRS[1]:
        for i in range(3):
            wind_copies[i, r].wait()
    for i in range(2):
        halo_copy(i).wait_recv()
    for k, r in enumerate(PAIRS[1]):
        advect(r, k)
    finish(1)

    for copy in weight_copies:
        copy.wait()
    w1t[...] = w1[...].T
    w2t[...] = w2[...].T
    w3t[...] = w3[...].T
    for src, dst in ((b1_line, b1), (b2_line, b2), (b3_line, b3)):
        for i in range(dst.shape[0] // 128):
            line = jnp.broadcast_to(src[i * 128 : (i + 1) * 128][None], (128, 128))
            dst[i * 128 : (i + 1) * 128, :] = line.T

    top = lax.broadcasted_iota(jnp.int32, (nlev, 128), 0) == 0

    def unpack(p):
        for off in ORDER:
            flux_copy(p, off).wait_recv()
            block_copy(p, off).wait_recv()
        for i, r in enumerate(PAIRS[p]):
            for pair in range(nfield // 2):
                pieces = ([], [])
                for g in range(16):
                    row = i * nfield * nlev + pair * 2 * nlev
                    both = recv[p, g, row : row + 2 * nlev].astype(jnp.float32)
                    for j in range(2):
                        piece = both[j * nlev : (j + 1) * nlev]
                        if g > 0:
                            k = i * nfield + 2 * pair + j
                            edge = flux_in[p, g - 1].astype(jnp.float32)[k : k + 1]
                            edge = jnp.broadcast_to(edge, (nlev, 128))
                            piece = piece + jnp.where(top, edge, 0.0)
                        pieces[j].append(piece)
                for j in range(2):
                    f = 2 * pair + j
                    whole = jnp.concatenate(pieces[j], axis=0)
                    ob[r, f * 128 : (f + 1) * 128] = whole
                    x_buf[f * 128 : (f + 1) * 128, i * 128 : (i + 1) * 128] = whole.astype(
                        jnp.bfloat16
                    )

    def twice(value):
        return jnp.concatenate([value, value], axis=1)

    def physics(p):
        ra, rb = PAIRS[p]
        x = x_buf[...]
        for start in range(0, 768, 256):
            rows = slice(start, start + 256)
            v = jnp.dot(w1t[rows], x, preferred_element_type=jnp.float32)
            h1[rows] = silu(v + twice(b1[rows])).astype(jnp.bfloat16)
        x = h1[...]
        for start in range(0, 640, 128):
            rows = slice(start, start + 128)
            v = jnp.dot(w2t[rows], x, preferred_element_type=jnp.float32)
            h2[rows] = silu(v + twice(b2[rows])).astype(jnp.bfloat16)
        x = h2[...]
        active = []
        for r in (ra, rb):
            hit = own_ref[0, 0, 0] == r
            for other in (own_ref[0, 0, 1], lent_ref[0, 0, 0], lent_ref[0, 0, 1]):
                hit = jnp.logical_or(hit, other == r)
            active.append(hit)
        for start in range(0, 512, 256):
            rows = slice(start, start + 256)
            v = jnp.dot(w3t[rows], x, preferred_element_type=jnp.float32)
            v = (v + twice(b3[rows])).astype(jnp.bfloat16).astype(jnp.float32)
            for i, r in enumerate((ra, rb)):
                out[pl.ds(start * nrow + r, 256, stride=nrow), :] = ob[r, rows] + jnp.where(
                    active[i], v[:, i * 128 : (i + 1) * 128], 0.0
                )

    for p in range(2):
        unpack(p)
        physics(p)

    for p in range(2):
        halo_copy(p).wait_send()
        for off in ORDER:
            flux_copy(p, off).wait_send()
            block_copy(p, off).wait_send()


ORDER = (8, 7, 9, 6, 10, 5, 11, 4, 12, 3, 13, 2, 14, 1, 15)


def in_hbm(value):
    return pltpu.with_memory_space_constraint(value, pltpu.HBM)


def body(
    fields,
    courant_lon,
    courant_lat,
    displacement,
    own_slot,
    lent_slot,
    w_first,
    bias_first,
    w_second,
    bias_second,
    w_third,
    bias_third,
):
    nfield, nlev, nrow, lon = fields.shape
    count = lax.axis_size("lev")
    width = nfield * nlev * count
    part = lon // count
    hidden = (w_first.shape[1], w_second.shape[1])
    f32, bf16 = jnp.float32, jnp.bfloat16
    hbm = pl.BlockSpec(memory_space=pltpu.HBM)
    dma = pltpu.SemaphoreType.DMA
    return pl.pallas_call(
        kernel,
        name="tracer",
        out_shape=jax.ShapeDtypeStruct((width * nrow, part), f32),
        in_specs=[hbm] * 12,
        out_specs=pl.BlockSpec(memory_space=pltpu.VMEM),
        scratch_shapes=[
            pltpu.VMEM((nfield, nrow, nlev, lon), f32),
            pltpu.VMEM((3, nrow, nlev, lon), f32),
            pltpu.VMEM((nfield, nrow, nlev, lon), f32),
            pltpu.VMEM((2, nfield // 2, 2 * nlev, lon), bf16),
            pltpu.VMEM((2, nfield // 2, 2 * nlev, lon), bf16),
            pltpu.VMEM((2 * nfield, lon), f32),
            pltpu.VMEM((2, count, 2 * nfield, part), bf16),
            pltpu.VMEM((2, count, 2 * nfield, part), bf16),
            pltpu.VMEM((2, count, 2 * nfield * nlev, part), bf16),
            pltpu.VMEM((2, count, 2 * nfield * nlev, part), bf16),
            pltpu.VMEM((width, hidden[0]), bf16),
            pltpu.VMEM((hidden[0], hidden[1]), bf16),
            pltpu.VMEM((hidden[1], width), bf16),
            pltpu.VMEM((hidden[0], width), bf16),
            pltpu.VMEM((hidden[1], hidden[0]), bf16),
            pltpu.VMEM((width, hidden[1]), bf16),
            pltpu.VMEM((hidden[0], 128), f32),
            pltpu.VMEM((hidden[1], 128), f32),
            pltpu.VMEM((width, 128), f32),
            pltpu.VMEM((nrow, width, part), f32),
            pltpu.VMEM((width, 2 * part), bf16),
            pltpu.VMEM((hidden[0], 2 * part), bf16),
            pltpu.VMEM((hidden[1], 2 * part), bf16),
            pltpu.SMEM(own_slot.shape, jnp.int32),
            pltpu.SMEM(lent_slot.shape, jnp.int32),
            pltpu.VMEM(bias_first.shape, f32),
            pltpu.VMEM(bias_second.shape, f32),
            pltpu.VMEM(bias_third.shape, f32),
            dma((nrow,)),
            dma((3, nrow)),
            dma((8,)),
            dma((2,)),
            dma((2,)),
            dma((2, count - 1)),
            dma((2, count - 1)),
            dma((2, count - 1)),
            dma((2, count - 1)),
        ],
        compiler_params=pltpu.CompilerParams(
            collective_id=0, has_side_effects=True, vmem_limit_bytes=48 << 20
        ),
    )(
        in_hbm(fields),
        in_hbm(courant_lon),
        in_hbm(courant_lat),
        in_hbm(displacement),
        in_hbm(own_slot),
        in_hbm(lent_slot),
        in_hbm(w_first),
        in_hbm(bias_first),
        in_hbm(w_second),
        in_hbm(bias_second),
        in_hbm(w_third),
        in_hbm(bias_third),
    ).reshape(width, nrow, part)


def solution(mesh):
    in_specs = (
        P(None, "lev", "lat", None),
        P("lev", "lat", None),
        P("lev", "lat", None),
        P("lev", "lat", None),
        P("lev", "lat", None),
        P("lev", "lat", None),
        P(),
        P(),
        P(),
        P(),
        P(),
        P(),
    )
    out_specs = P(None, "lat", "lev")
    return jax.shard_map(body, mesh=mesh, in_specs=in_specs, out_specs=out_specs, check_vma=False)
```

```python
import jax
import jax.numpy as jnp
from jax import lax
from jax.experimental import pallas as pl
from jax.experimental.pallas import tpu as pltpu
from jax.sharding import PartitionSpec as P

MESH = pl.DeviceIdType.MESH
STAGES = ((1, 2), (3,), (0,))


def silu(value):
    return value * (0.5 + 0.5 * jnp.tanh(0.5 * value))


def kernel(
    fields_hbm,
    lon_hbm,
    lat_hbm,
    move_hbm,
    own_hbm,
    lent_hbm,
    w1_hbm,
    b1_hbm,
    w2_hbm,
    b2_hbm,
    w3_hbm,
    b3_hbm,
    out,
    fb,
    cb,
    part,
    halo_out,
    halo_in,
    flux_row,
    *refs,
):
    buffers, refs = refs[: 4 * len(STAGES)], refs[4 * len(STAGES) :]
    flux_out, flux_in, send, recv = (buffers[k :: 4] for k in range(4))
    (
        w1,
        w2,
        w3,
        w1t,
        w2t,
        w3t,
        b1,
        b2,
        b3,
        ob,
        x_buf,
        h1,
        h2,
        own_ref,
        lent_ref,
        b1_line,
        b2_line,
        b3_line,
        field_sem,
        wind_sem,
        weight_sem,
        halo_send_sem,
        halo_recv_sem,
        ready_lat,
        ready_lev,
        flux_send_sem,
        flux_recv_sem,
        send_sem,
        recv_sem,
    ) = refs
    count = lax.axis_size("lev")
    bands = lax.axis_size("lat")
    lev = lax.axis_index("lev")
    lat = lax.axis_index("lat")
    north, south = lax.rem(lat + bands - 1, bands), lax.rem(lat + 1, bands)
    nfield, nrow, nlev, lon = fb.shape

    field_copies = {}
    wind_copies = {}
    for r in (0, 3, 1, 2):
        field_copies[r] = pltpu.make_async_copy(
            fields_hbm.at[:, :, r, :], fb.at[:, r], field_sem.at[r]
        )
        field_copies[r].start()
    for r in (1, 2, 0, 3):
        for i, src in enumerate((lon_hbm, lat_hbm, move_hbm)):
            wind_copies[i, r] = pltpu.make_async_copy(
                src.at[:, r, :], cb.at[i, r], wind_sem.at[i, r]
            )
            wind_copies[i, r].start()
    weight_copies = []
    moves = (
        (w1_hbm, w1),
        (b1_hbm, b1_line),
        (b2_hbm, b2_line),
        (b3_hbm, b3_line),
        (own_hbm, own_ref),
        (lent_hbm, lent_ref),
        (w2_hbm, w2),
        (w3_hbm, w3),
    )
    for i, (src, dst) in enumerate(moves):
        weight_copies.append(pltpu.make_async_copy(src, dst, weight_sem.at[i]))

    first_band = lat == 0
    last_band = lat == bands - 1
    late_owner = jnp.logical_and(first_band, lev == 0)
    late_peer = jnp.logical_and(first_band, lev != 0)

    barrier = pltpu.get_barrier_semaphore()

    @pl.when(jnp.logical_not(late_owner))
    def _():
        for off in ORDER:
            target = lax.rem(lev + off, count)
            pl.semaphore_signal(barrier, 1, device_id={"lev": target}, device_id_type=MESH)

    @pl.when(jnp.logical_not(first_band))
    def _():
        pl.semaphore_signal(barrier, 1, device_id={"lat": north}, device_id_type=MESH)

    @pl.when(first_band)
    def _():
        halo_in[0] = jnp.zeros(halo_in.shape[1:], halo_in.dtype)

    @pl.when(last_band)
    def _():
        halo_in[1] = jnp.zeros(halo_in.shape[1:], halo_in.dtype)

    sub = lax.broadcasted_iota(jnp.int32, (nlev, lon), 0)

    def advect(r, k):
        lonp = jnp.maximum(cb[0, r], 0.0)
        lonn = jnp.minimum(cb[0, r], 0.0)
        latp = jnp.maximum(cb[1, r], 0.0)
        latn = jnp.minimum(cb[1, r], 0.0)
        move = cb[2, r]
        last = jnp.logical_and(sub == nlev - 1, lev == count - 1)
        move = jnp.where(last, 0.0, move)
        for f in range(nfield):
            x = fb[f, r]
            if r == 0:
                up = halo_in[0, f // 2].astype(jnp.float32)
                up = up[(f % 2) * nlev : (f % 2 + 1) * nlev]
            else:
                up = fb[f, r - 1]
            if r == nrow - 1:
                down = halo_in[1, f // 2].astype(jnp.float32)
                down = down[(f % 2) * nlev : (f % 2 + 1) * nlev]
            else:
                down = fb[f, r + 1]
            value = x - lonp * (x - pltpu.roll(x, 1, 1))
            value = value - lonn * (pltpu.roll(x, lon - 1, 1) - x)
            value = value - latp * (x - up)
            value = value - latn * (down - x)
            flux = move * value
            turned = pltpu.roll(flux, 1, 0)
            part[f, r] = value - flux + jnp.where(sub == 0, 0.0, turned)
            flux_row[k * nfield + f : k * nfield + f + 1, :] = turned[0:1]

    def flux_copy(p, off):
        target = lax.rem(lev + off, count)
        return pltpu.make_async_remote_copy(
            src_ref=flux_out[p].at[target],
            dst_ref=flux_in[p].at[lev],
            send_sem=flux_send_sem.at[p, off - 1],
            recv_sem=flux_recv_sem.at[p, off - 1],
            device_id={"lev": target},
            device_id_type=MESH,
        )

    def halo_copy(i):
        return pltpu.make_async_remote_copy(
            src_ref=halo_out.at[i],
            dst_ref=halo_in.at[i],
            send_sem=halo_send_sem.at[i],
            recv_sem=halo_recv_sem.at[i],
            device_id={"lat": south if i == 0 else north},
            device_id_type=MESH,
        )

    def block_copy(p, off):
        target = lax.rem(lev + off, count)
        return pltpu.make_async_remote_copy(
            src_ref=send[p].at[target],
            dst_ref=recv[p].at[lev],
            send_sem=send_sem.at[p, off - 1],
            recv_sem=recv_sem.at[p, off - 1],
            device_id={"lev": target},
            device_id_type=MESH,
        )

    def finish(p):
        for i, r in enumerate(STAGES[p]):
            for pair in range(nfield // 2):
                both = jnp.concatenate([part[2 * pair, r], part[2 * pair + 1, r]], axis=0)
                both = both.astype(jnp.bfloat16)
                row = i * nfield * nlev + pair * 2 * nlev
                for g in range(16):
                    send[p][g, row : row + 2 * nlev, :] = both[:, g * 128 : (g + 1) * 128]
        edge = flux_row[0 : len(STAGES[p]) * nfield]
        for g in range(16):
            flux_out[p][g] = edge[:, g * 128 : (g + 1) * 128]
        for off in ORDER:
            late = jnp.logical_and(first_band, lax.rem(lev + off, count) == 0)

            @pl.when(jnp.logical_not(late))
            def _():
                flux_copy(p, off).start()
                block_copy(p, off).start()

        recv[p][lev] = send[p][lev]
        flux_in[p][lev] = flux_out[p][lev]

    field_copies[0].wait()
    field_copies[3].wait()
    for i, r in ((0, 3), (1, 0)):
        for pair in range(nfield // 2):
            both = jnp.concatenate([fb[2 * pair, r], fb[2 * pair + 1, r]], axis=0)
            halo_out[i, pair] = both.astype(jnp.bfloat16)
    field_copies[1].wait()
    field_copies[2].wait()
    for k, r in enumerate(STAGES[0]):
        for i in range(3):
            wind_copies[i, r].wait()
        advect(r, k)
    for copy in weight_copies:
        copy.start()

    arrivals = count - 1 - late_peer.astype(jnp.int32) + 1 - last_band.astype(jnp.int32)
    pl.semaphore_wait(barrier, arrivals)

    @pl.when(jnp.logical_not(last_band))
    def _():
        halo_copy(0).start()
        pl.semaphore_signal(ready_lat, 1, device_id={"lat": south}, device_id_type=MESH)

    @pl.when(late_owner)
    def _():
        for off in ORDER:
            target = lax.rem(lev + off, count)
            pl.semaphore_signal(ready_lev, 1, device_id={"lev": target}, device_id_type=MESH)

    finish(0)

    for copy in weight_copies:
        copy.wait()
    w1t[...] = w1[...].T
    w2t[...] = w2[...].T
    w3t[...] = w3[...].T
    for src, dst in ((b1_line, b1), (b2_line, b2), (b3_line, b3)):
        for i in range(dst.shape[0] // 128):
            line = jnp.broadcast_to(src[i * 128 : (i + 1) * 128][None], (128, 128))
            dst[i * 128 : (i + 1) * 128, :] = line.T

    @pl.when(jnp.logical_not(first_band))
    def _():
        pl.semaphore_wait(ready_lat, 1)
        halo_copy(1).start()

    for i in range(3):
        wind_copies[i, 3].wait()

    @pl.when(jnp.logical_not(last_band))
    def _():
        halo_copy(1).wait_recv()

    advect(3, 0)
    finish(1)
    for i in range(3):
        wind_copies[i, 0].wait()

    @pl.when(jnp.logical_not(first_band))
    def _():
        halo_copy(0).wait_recv()

    advect(0, 0)
    finish(2)

    @pl.when(late_peer)
    def _():
        pl.semaphore_wait(ready_lev, 1)
        for p in range(len(STAGES)):
            flux_copy(p, count - lev).start()
            block_copy(p, count - lev).start()

    top = lax.broadcasted_iota(jnp.int32, (nlev, 128), 0) == 0

    def unpack(p):
        for off in ORDER:
            flux_copy(p, off).wait_recv()
            block_copy(p, off).wait_recv()
        for i, r in enumerate(STAGES[p]):
            for pair in range(nfield // 2):
                pieces = ([], [])
                for g in range(16):
                    row = i * nfield * nlev + pair * 2 * nlev
                    both = recv[p][g, row : row + 2 * nlev].astype(jnp.float32)
                    for j in range(2):
                        piece = both[j * nlev : (j + 1) * nlev]
                        if g > 0:
                            k = i * nfield + 2 * pair + j
                            edge = flux_in[p][g - 1, k : k + 1, :]
                            edge = jnp.broadcast_to(edge, (nlev, 128))
                            piece = piece + jnp.where(top, edge, 0.0)
                        pieces[j].append(piece)
                for j in range(2):
                    f = 2 * pair + j
                    whole = jnp.concatenate(pieces[j], axis=0)
                    ob[r, f * 128 : (f + 1) * 128] = whole
                    x_buf[f * 128 : (f + 1) * 128, i * 128 : (i + 1) * 128] = whole.astype(
                        jnp.bfloat16
                    )

    def physics(p):
        rows = STAGES[p]
        cols = 128 * len(rows)

        def wide(value):
            return jnp.concatenate([value] * len(rows), axis=1)

        x = x_buf[:, 0:cols]
        for start in range(0, 768, 256):
            span = slice(start, start + 256)
            v = jnp.dot(w1t[span], x, preferred_element_type=jnp.float32)
            h1[span, 0:cols] = silu(v + wide(b1[span])).astype(jnp.bfloat16)
        x = h1[:, 0:cols]
        for start in range(0, 640, 128):
            span = slice(start, start + 128)
            v = jnp.dot(w2t[span], x, preferred_element_type=jnp.float32)
            h2[span, 0:cols] = silu(v + wide(b2[span])).astype(jnp.bfloat16)
        x = h2[:, 0:cols]
        active = []
        for r in rows:
            hit = own_ref[0, 0, 0] == r
            for other in (own_ref[0, 0, 1], lent_ref[0, 0, 0], lent_ref[0, 0, 1]):
                hit = jnp.logical_or(hit, other == r)
            active.append(hit)
        for start in range(0, 512, 256):
            span = slice(start, start + 256)
            v = jnp.dot(w3t[span], x, preferred_element_type=jnp.float32)
            v = (v + wide(b3[span])).astype(jnp.bfloat16).astype(jnp.float32)
            for i, r in enumerate(rows):
                out[pl.ds(start * nrow + r, 256, stride=nrow), :] = ob[r, span] + jnp.where(
                    active[i], v[:, i * 128 : (i + 1) * 128], 0.0
                )

    for p in range(len(STAGES)):
        unpack(p)
        physics(p)

    @pl.when(jnp.logical_not(last_band))
    def _():
        halo_copy(0).wait_send()

    @pl.when(jnp.logical_not(first_band))
    def _():
        halo_copy(1).wait_send()

    for p in range(len(STAGES)):
        for off in ORDER:
            flux_copy(p, off).wait_send()
            block_copy(p, off).wait_send()


ORDER = (8, 7, 9, 6, 10, 5, 11, 4, 12, 3, 13, 2, 14, 1, 15)


def in_hbm(value):
    return pltpu.with_memory_space_constraint(value, pltpu.HBM)


def body(
    fields,
    courant_lon,
    courant_lat,
    displacement,
    own_slot,
    lent_slot,
    w_first,
    bias_first,
    w_second,
    bias_second,
    w_third,
    bias_third,
):
    nfield, nlev, nrow, lon = fields.shape
    count = lax.axis_size("lev")
    width = nfield * nlev * count
    part = lon // count
    hidden = (w_first.shape[1], w_second.shape[1])
    f32, bf16 = jnp.float32, jnp.bfloat16
    hbm = pl.BlockSpec(memory_space=pltpu.HBM)
    dma = pltpu.SemaphoreType.DMA
    stages = len(STAGES)
    buffers = []
    for rows in STAGES:
        buffers += [pltpu.VMEM((count, len(rows) * nfield, part), f32)] * 2
        buffers += [pltpu.VMEM((count, len(rows) * nfield * nlev, part), bf16)] * 2
    return pl.pallas_call(
        kernel,
        name="tracer",
        out_shape=jax.ShapeDtypeStruct((width * nrow, part), f32),
        in_specs=[hbm] * 12,
        out_specs=pl.BlockSpec(memory_space=pltpu.VMEM),
        scratch_shapes=[
            pltpu.VMEM((nfield, nrow, nlev, lon), f32),
            pltpu.VMEM((3, nrow, nlev, lon), f32),
            pltpu.VMEM((nfield, nrow, nlev, lon), f32),
            pltpu.VMEM((2, nfield // 2, 2 * nlev, lon), bf16),
            pltpu.VMEM((2, nfield // 2, 2 * nlev, lon), bf16),
            pltpu.VMEM((2 * nfield, lon), f32),
            *buffers,
            pltpu.VMEM((width, hidden[0]), bf16),
            pltpu.VMEM((hidden[0], hidden[1]), bf16),
            pltpu.VMEM((hidden[1], width), bf16),
            pltpu.VMEM((hidden[0], width), bf16),
            pltpu.VMEM((hidden[1], hidden[0]), bf16),
            pltpu.VMEM((width, hidden[1]), bf16),
            pltpu.VMEM((hidden[0], 128), f32),
            pltpu.VMEM((hidden[1], 128), f32),
            pltpu.VMEM((width, 128), f32),
            pltpu.VMEM((nrow, width, part), f32),
            pltpu.VMEM((width, 2 * part), bf16),
            pltpu.VMEM((hidden[0], 2 * part), bf16),
            pltpu.VMEM((hidden[1], 2 * part), bf16),
            pltpu.SMEM(own_slot.shape, jnp.int32),
            pltpu.SMEM(lent_slot.shape, jnp.int32),
            pltpu.VMEM(bias_first.shape, f32),
            pltpu.VMEM(bias_second.shape, f32),
            pltpu.VMEM(bias_third.shape, f32),
            dma((nrow,)),
            dma((3, nrow)),
            dma((8,)),
            dma((2,)),
            dma((2,)),
            pltpu.SemaphoreType.REGULAR,
            pltpu.SemaphoreType.REGULAR,
            dma((stages, count - 1)),
            dma((stages, count - 1)),
            dma((stages, count - 1)),
            dma((stages, count - 1)),
        ],
        compiler_params=pltpu.CompilerParams(
            collective_id=0, has_side_effects=True, vmem_limit_bytes=48 << 20
        ),
    )(
        in_hbm(fields),
        in_hbm(courant_lon),
        in_hbm(courant_lat),
        in_hbm(displacement),
        in_hbm(own_slot),
        in_hbm(lent_slot),
        in_hbm(w_first),
        in_hbm(bias_first),
        in_hbm(w_second),
        in_hbm(bias_second),
        in_hbm(w_third),
        in_hbm(bias_third),
    ).reshape(width, nrow, part)


def solution(mesh):
    in_specs = (
        P(None, "lev", "lat", None),
        P("lev", "lat", None),
        P("lev", "lat", None),
        P("lev", "lat", None),
        P("lev", "lat", None),
        P("lev", "lat", None),
        P(),
        P(),
        P(),
        P(),
        P(),
        P(),
    )
    out_specs = P(None, "lat", "lev")
    return jax.shard_map(body, mesh=mesh, in_specs=in_specs, out_specs=out_specs, check_vma=False)
```

```python
import jax
import jax.numpy as jnp
from jax import lax
from jax.experimental import pallas as pl
from jax.experimental.pallas import tpu as pltpu
from jax.sharding import PartitionSpec as P

MESH = pl.DeviceIdType.MESH
STAGES = ((1, 2), (3,), (0,))


def silu(value):
    return value * (0.5 + 0.5 * jnp.tanh(0.5 * value))


def kernel(
    fields_hbm,
    lon_hbm,
    lat_hbm,
    move_hbm,
    own_hbm,
    lent_hbm,
    w1_hbm,
    b1_hbm,
    w2_hbm,
    b2_hbm,
    w3_hbm,
    b3_hbm,
    out,
    fb,
    cb,
    part,
    halo_out,
    halo_in,
    flux_row,
    *refs,
):
    buffers, refs = refs[: 4 * len(STAGES)], refs[4 * len(STAGES) :]
    flux_out, flux_in, send, recv = (buffers[k :: 4] for k in range(4))
    (
        w1,
        w2,
        w3,
        w1t,
        w2t,
        w3t,
        b1,
        b2,
        b3,
        ob,
        x_buf,
        h1,
        h2,
        own_ref,
        lent_ref,
        b1_line,
        b2_line,
        b3_line,
        field_sem,
        wind_sem,
        weight_sem,
        halo_send_sem,
        halo_recv_sem,
        ready_lat,
        ready_lev,
        flux_send_sem,
        flux_recv_sem,
        send_sem,
        recv_sem,
    ) = refs
    count = lax.axis_size("lev")
    bands = lax.axis_size("lat")
    lev = lax.axis_index("lev")
    lat = lax.axis_index("lat")
    north, south = lax.rem(lat + bands - 1, bands), lax.rem(lat + 1, bands)
    nfield, nrow, nlev, lon = fb.shape

    field_copies = {}
    wind_copies = {}
    for r in (0, 3, 1, 2):
        field_copies[r] = pltpu.make_async_copy(
            fields_hbm.at[:, :, r, :], fb.at[:, r], field_sem.at[r]
        )
        field_copies[r].start()
    for r in (1, 2, 0, 3):
        for i, src in enumerate((lon_hbm, lat_hbm, move_hbm)):
            wind_copies[i, r] = pltpu.make_async_copy(
                src.at[:, r, :], cb.at[i, r], wind_sem.at[i, r]
            )
            wind_copies[i, r].start()
    weight_copies = []
    moves = (
        (w1_hbm, w1),
        (b1_hbm, b1_line),
        (b2_hbm, b2_line),
        (b3_hbm, b3_line),
        (own_hbm, own_ref),
        (lent_hbm, lent_ref),
        (w2_hbm, w2),
        (w3_hbm, w3),
    )
    for i, (src, dst) in enumerate(moves):
        weight_copies.append(pltpu.make_async_copy(src, dst, weight_sem.at[i]))

    first_band = lat == 0
    last_band = lat == bands - 1
    late_owner = jnp.logical_and(first_band, lev == 0)
    late_peer = jnp.logical_and(first_band, lev != 0)

    barrier = pltpu.get_barrier_semaphore()

    @pl.when(jnp.logical_not(late_owner))
    def _():
        for off in ORDER:
            target = lax.rem(lev + off, count)
            pl.semaphore_signal(barrier, 1, device_id={"lev": target}, device_id_type=MESH)

    @pl.when(jnp.logical_not(first_band))
    def _():
        pl.semaphore_signal(barrier, 1, device_id={"lat": north}, device_id_type=MESH)

    @pl.when(first_band)
    def _():
        halo_in[0] = jnp.zeros(halo_in.shape[1:], halo_in.dtype)

    @pl.when(last_band)
    def _():
        halo_in[1] = jnp.zeros(halo_in.shape[1:], halo_in.dtype)

    sub = lax.broadcasted_iota(jnp.int32, (nlev, lon), 0)

    def halo_tile(i, f, g):
        rows = slice((f % 2) * nlev, (f % 2 + 1) * nlev)
        tile = halo_in[i, g % 2, f // 2, :, (g // 2) * 128 : (g // 2 + 1) * 128]
        return tile.astype(jnp.float32)[rows]

    def moved(r, cols):
        last = jnp.logical_and(sub[:, cols] == nlev - 1, lev == count - 1)
        return jnp.where(last, 0.0, cb[2, r, :, cols])

    def advect(r, k):
        lonp = jnp.maximum(cb[0, r], 0.0)
        lonn = jnp.minimum(cb[0, r], 0.0)
        latp = jnp.maximum(cb[1, r], 0.0)
        latn = jnp.minimum(cb[1, r], 0.0)
        move = moved(r, slice(None))
        for f in range(nfield):
            x = fb[f, r]
            if r == nrow - 1:
                down = jnp.concatenate([halo_tile(1, f, g) for g in range(16)], axis=1)
            else:
                down = fb[f, r + 1]
            value = x - lonp * (x - pltpu.roll(x, 1, 1))
            value = value - lonn * (pltpu.roll(x, lon - 1, 1) - x)
            if r == 0:
                part[f, r] = value - latn * (down - x)
                continue
            value = value - latp * (x - fb[f, r - 1])
            value = value - latn * (down - x)
            flux = move * value
            turned = pltpu.roll(flux, 1, 0)
            part[f, r] = value - flux + jnp.where(sub == 0, 0.0, turned)
            flux_row[k * nfield + f : k * nfield + f + 1, :] = turned[0:1]

    def north_row(half):
        for g in range(half, 16, 2):
            cols = slice(g * 128, (g + 1) * 128)
            level = sub[:, cols]
            latp = jnp.maximum(cb[1, 0, :, cols], 0.0)
            move = moved(0, cols)
            edge = jnp.zeros((nlev, 128), jnp.float32)
            for pair in range(nfield // 2):
                values = []
                for f in (2 * pair, 2 * pair + 1):
                    x = fb[f, 0, :, cols]
                    value = part[f, 0, :, cols] - latp * (x - halo_tile(0, f, g))
                    flux = move * value
                    turned = pltpu.roll(flux, 1, 0)
                    values.append(value - flux + jnp.where(level == 0, 0.0, turned))
                    edge = jnp.where(level == f, pltpu.roll(flux, f + 1, 0), edge)
                both = jnp.concatenate(values, axis=0).astype(jnp.bfloat16)
                send[2][g, pair * 2 * nlev : (pair + 1) * 2 * nlev, :] = both
            flux_out[2][g] = edge[0:nfield].astype(jnp.bfloat16)

    def flux_copy(p, off):
        target = lax.rem(lev + off, count)
        return pltpu.make_async_remote_copy(
            src_ref=flux_out[p].at[target],
            dst_ref=flux_in[p].at[lev],
            send_sem=flux_send_sem.at[p, off - 1],
            recv_sem=flux_recv_sem.at[p, off - 1],
            device_id={"lev": target},
            device_id_type=MESH,
        )

    def halo_copy(i, half):
        return pltpu.make_async_remote_copy(
            src_ref=halo_out.at[i, half],
            dst_ref=halo_in.at[i, half],
            send_sem=halo_send_sem.at[i, half],
            recv_sem=halo_recv_sem.at[i, half],
            device_id={"lat": south if i == 0 else north},
            device_id_type=MESH,
        )

    def block_copy(p, off):
        target = lax.rem(lev + off, count)
        return pltpu.make_async_remote_copy(
            src_ref=send[p].at[target],
            dst_ref=recv[p].at[lev],
            send_sem=send_sem.at[p, off - 1],
            recv_sem=recv_sem.at[p, off - 1],
            device_id={"lev": target},
            device_id_type=MESH,
        )

    def finish(p):
        for i, r in enumerate(STAGES[p]):
            for pair in range(nfield // 2):
                both = jnp.concatenate([part[2 * pair, r], part[2 * pair + 1, r]], axis=0)
                both = both.astype(jnp.bfloat16)
                row = i * nfield * nlev + pair * 2 * nlev
                for g in range(16):
                    send[p][g, row : row + 2 * nlev, :] = both[:, g * 128 : (g + 1) * 128]
        edge = flux_row[0 : len(STAGES[p]) * nfield].astype(jnp.bfloat16)
        for g in range(16):
            flux_out[p][g] = edge[:, g * 128 : (g + 1) * 128]
        launch(p, (0, 1))

    def launch(p, halves):
        for off in ORDER:
            target = lax.rem(lev + off, count)
            wanted = jnp.logical_not(jnp.logical_and(first_band, target == 0))
            if len(halves) == 1:
                wanted = jnp.logical_and(wanted, lax.rem(target, 2) == halves[0])

            @pl.when(wanted)
            def _():
                flux_copy(p, off).start()
                block_copy(p, off).start()

    field_copies[0].wait()
    field_copies[3].wait()
    for i, r in ((0, 3), (1, 0)):
        for pair in range(nfield // 2):
            both = jnp.concatenate([fb[2 * pair, r], fb[2 * pair + 1, r]], axis=0)
            both = both.astype(jnp.bfloat16)
            for g in range(16):
                halo_out[i, g % 2, pair, :, (g // 2) * 128 : (g // 2 + 1) * 128] = both[
                    :, g * 128 : (g + 1) * 128
                ]

    arrivals = count - 1 - late_peer.astype(jnp.int32) + 1 - last_band.astype(jnp.int32)
    pl.semaphore_wait(barrier, arrivals)

    @pl.when(jnp.logical_not(last_band))
    def _():
        for half in range(2):
            halo_copy(0, half).start()
        pl.semaphore_signal(ready_lat, 1, device_id={"lat": south}, device_id_type=MESH)

    @pl.when(late_owner)
    def _():
        for off in ORDER:
            target = lax.rem(lev + off, count)
            pl.semaphore_signal(ready_lev, 1, device_id={"lev": target}, device_id_type=MESH)

    field_copies[1].wait()
    field_copies[2].wait()
    for k, r in enumerate(STAGES[0]):
        for i in range(3):
            wind_copies[i, r].wait()
        advect(r, k)
    finish(0)

    for copy in weight_copies:
        copy.start()
    for i in range(3):
        wind_copies[i, 0].wait()
    advect(0, 0)
    for copy in weight_copies:
        copy.wait()
    w1t[...] = w1[...].T
    w2t[...] = w2[...].T
    w3t[...] = w3[...].T
    for src, dst in ((b1_line, b1), (b2_line, b2), (b3_line, b3)):
        for i in range(dst.shape[0] // 128):
            line = jnp.broadcast_to(src[i * 128 : (i + 1) * 128][None], (128, 128))
            dst[i * 128 : (i + 1) * 128, :] = line.T

    @pl.when(jnp.logical_not(first_band))
    def _():
        pl.semaphore_wait(ready_lat, 1)
        for half in range(2):
            halo_copy(1, half).start()

    for i in range(3):
        wind_copies[i, 3].wait()

    @pl.when(jnp.logical_not(last_band))
    def _():
        for half in range(2):
            halo_copy(1, half).wait_recv()

    advect(3, 0)
    finish(1)
    for half in range(2):

        @pl.when(jnp.logical_not(first_band))
        def _():
            halo_copy(0, half).wait_recv()

        north_row(half)
        launch(2, (half,))

    @pl.when(late_peer)
    def _():
        pl.semaphore_wait(ready_lev, 1)
        for p in range(len(STAGES)):
            flux_copy(p, count - lev).start()
            block_copy(p, count - lev).start()

    top = lax.broadcasted_iota(jnp.int32, (nlev, 128), 0) == 0

    def unpack(p):
        recv[p][lev] = send[p][lev]
        flux_in[p][lev] = flux_out[p][lev]
        for off in ORDER:
            flux_copy(p, off).wait_recv()
            block_copy(p, off).wait_recv()
        for i, r in enumerate(STAGES[p]):
            for pair in range(nfield // 2):
                pieces = ([], [])
                for g in range(16):
                    row = i * nfield * nlev + pair * 2 * nlev
                    both = recv[p][g, row : row + 2 * nlev].astype(jnp.float32)
                    for j in range(2):
                        piece = both[j * nlev : (j + 1) * nlev]
                        if g > 0:
                            k = i * nfield + 2 * pair + j
                            edge = flux_in[p][g - 1].astype(jnp.float32)[k : k + 1]
                            edge = jnp.broadcast_to(edge, (nlev, 128))
                            piece = piece + jnp.where(top, edge, 0.0)
                        pieces[j].append(piece)
                for j in range(2):
                    f = 2 * pair + j
                    whole = jnp.concatenate(pieces[j], axis=0)
                    ob[r, f * 128 : (f + 1) * 128] = whole
                    x_buf[f * 128 : (f + 1) * 128, i * 128 : (i + 1) * 128] = whole.astype(
                        jnp.bfloat16
                    )

    def physics(p):
        rows = STAGES[p]
        cols = 128 * len(rows)

        def wide(value):
            return jnp.concatenate([value] * len(rows), axis=1)

        x = x_buf[:, 0:cols]
        for start in range(0, 768, 256):
            span = slice(start, start + 256)
            v = jnp.dot(w1t[span], x, preferred_element_type=jnp.float32)
            h1[span, 0:cols] = silu(v + wide(b1[span])).astype(jnp.bfloat16)
        x = h1[:, 0:cols]
        for start in range(0, 640, 128):
            span = slice(start, start + 128)
            v = jnp.dot(w2t[span], x, preferred_element_type=jnp.float32)
            h2[span, 0:cols] = silu(v + wide(b2[span])).astype(jnp.bfloat16)
        x = h2[:, 0:cols]
        active = []
        for r in rows:
            hit = own_ref[0, 0, 0] == r
            for other in (own_ref[0, 0, 1], lent_ref[0, 0, 0], lent_ref[0, 0, 1]):
                hit = jnp.logical_or(hit, other == r)
            active.append(hit)
        for start in range(0, 512, 256):
            span = slice(start, start + 256)
            v = jnp.dot(w3t[span], x, preferred_element_type=jnp.float32)
            v = (v + wide(b3[span])).astype(jnp.bfloat16).astype(jnp.float32)
            for i, r in enumerate(rows):
                out[pl.ds(start * nrow + r, 256, stride=nrow), :] = ob[r, span] + jnp.where(
                    active[i], v[:, i * 128 : (i + 1) * 128], 0.0
                )

    for p in range(len(STAGES)):
        unpack(p)
        physics(p)

    @pl.when(jnp.logical_not(last_band))
    def _():
        for half in range(2):
            halo_copy(0, half).wait_send()

    @pl.when(jnp.logical_not(first_band))
    def _():
        for half in range(2):
            halo_copy(1, half).wait_send()

    for p in range(len(STAGES)):
        for off in ORDER:
            flux_copy(p, off).wait_send()
            block_copy(p, off).wait_send()


ORDER = (8, 7, 9, 6, 10, 5, 11, 4, 12, 3, 13, 2, 14, 1, 15)


def in_hbm(value):
    return pltpu.with_memory_space_constraint(value, pltpu.HBM)


def body(
    fields,
    courant_lon,
    courant_lat,
    displacement,
    own_slot,
    lent_slot,
    w_first,
    bias_first,
    w_second,
    bias_second,
    w_third,
    bias_third,
):
    nfield, nlev, nrow, lon = fields.shape
    count = lax.axis_size("lev")
    width = nfield * nlev * count
    part = lon // count
    hidden = (w_first.shape[1], w_second.shape[1])
    f32, bf16 = jnp.float32, jnp.bfloat16
    hbm = pl.BlockSpec(memory_space=pltpu.HBM)
    dma = pltpu.SemaphoreType.DMA
    stages = len(STAGES)
    buffers = []
    for rows in STAGES:
        buffers += [pltpu.VMEM((count, len(rows) * nfield, part), bf16)] * 2
        buffers += [pltpu.VMEM((count, len(rows) * nfield * nlev, part), bf16)] * 2
    return pl.pallas_call(
        kernel,
        name="tracer",
        out_shape=jax.ShapeDtypeStruct((width * nrow, part), f32),
        in_specs=[hbm] * 12,
        out_specs=pl.BlockSpec(memory_space=pltpu.VMEM),
        scratch_shapes=[
            pltpu.VMEM((nfield, nrow, nlev, lon), f32),
            pltpu.VMEM((3, nrow, nlev, lon), f32),
            pltpu.VMEM((nfield, nrow, nlev, lon), f32),
            pltpu.VMEM((2, 2, nfield // 2, 2 * nlev, lon // 2), bf16),
            pltpu.VMEM((2, 2, nfield // 2, 2 * nlev, lon // 2), bf16),
            pltpu.VMEM((2 * nfield, lon), f32),
            *buffers,
            pltpu.VMEM((width, hidden[0]), bf16),
            pltpu.VMEM((hidden[0], hidden[1]), bf16),
            pltpu.VMEM((hidden[1], width), bf16),
            pltpu.VMEM((hidden[0], width), bf16),
            pltpu.VMEM((hidden[1], hidden[0]), bf16),
            pltpu.VMEM((width, hidden[1]), bf16),
            pltpu.VMEM((hidden[0], 128), f32),
            pltpu.VMEM((hidden[1], 128), f32),
            pltpu.VMEM((width, 128), f32),
            pltpu.VMEM((nrow, width, part), f32),
            pltpu.VMEM((width, 2 * part), bf16),
            pltpu.VMEM((hidden[0], 2 * part), bf16),
            pltpu.VMEM((hidden[1], 2 * part), bf16),
            pltpu.SMEM(own_slot.shape, jnp.int32),
            pltpu.SMEM(lent_slot.shape, jnp.int32),
            pltpu.VMEM(bias_first.shape, f32),
            pltpu.VMEM(bias_second.shape, f32),
            pltpu.VMEM(bias_third.shape, f32),
            dma((nrow,)),
            dma((3, nrow)),
            dma((8,)),
            dma((2, 2)),
            dma((2, 2)),
            pltpu.SemaphoreType.REGULAR,
            pltpu.SemaphoreType.REGULAR,
            dma((stages, count - 1)),
            dma((stages, count - 1)),
            dma((stages, count - 1)),
            dma((stages, count - 1)),
        ],
        compiler_params=pltpu.CompilerParams(
            collective_id=0, has_side_effects=True, vmem_limit_bytes=48 << 20
        ),
    )(
        in_hbm(fields),
        in_hbm(courant_lon),
        in_hbm(courant_lat),
        in_hbm(displacement),
        in_hbm(own_slot),
        in_hbm(lent_slot),
        in_hbm(w_first),
        in_hbm(bias_first),
        in_hbm(w_second),
        in_hbm(bias_second),
        in_hbm(w_third),
        in_hbm(bias_third),
    ).reshape(width, nrow, part)


def solution(mesh):
    in_specs = (
        P(None, "lev", "lat", None),
        P("lev", "lat", None),
        P("lev", "lat", None),
        P("lev", "lat", None),
        P("lev", "lat", None),
        P("lev", "lat", None),
        P(),
        P(),
        P(),
        P(),
        P(),
        P(),
    )
    out_specs = P(None, "lat", "lev")
    return jax.shard_map(body, mesh=mesh, in_specs=in_specs, out_specs=out_specs, check_vma=False)
```

```python
import jax
import jax.numpy as jnp
from jax import lax
from jax.experimental import pallas as pl
from jax.experimental.pallas import tpu as pltpu
from jax.sharding import PartitionSpec as P

MESH = pl.DeviceIdType.MESH
STAGES = ((1, 2), (3,), (0,))


def silu(value):
    return value * (0.5 + 0.5 * jnp.tanh(0.5 * value))


def kernel(
    fields_hbm,
    lon_hbm,
    lat_hbm,
    move_hbm,
    own_hbm,
    lent_hbm,
    w1_hbm,
    b1_hbm,
    w2_hbm,
    b2_hbm,
    w3_hbm,
    b3_hbm,
    out,
    fb,
    cb,
    part,
    halo_out,
    halo_in,
    flux_row,
    *refs,
):
    buffers, refs = refs[: 4 * len(STAGES)], refs[4 * len(STAGES) :]
    flux_out, flux_in, send, recv = (buffers[k :: 4] for k in range(4))
    (
        w1,
        w2,
        w3,
        w1t,
        w2t,
        w3t,
        b1,
        b2,
        b3,
        ob,
        x_buf,
        h1,
        h2,
        own_ref,
        lent_ref,
        b1_line,
        b2_line,
        b3_line,
        field_sem,
        wind_sem,
        weight_sem,
        halo_send_sem,
        halo_recv_sem,
        ready_north,
        ready_south,
        ready_lev,
        flux_send_sem,
        flux_recv_sem,
        send_sem,
        recv_sem,
    ) = refs
    count = lax.axis_size("lev")
    bands = lax.axis_size("lat")
    lev = lax.axis_index("lev")
    lat = lax.axis_index("lat")
    north, south = lax.rem(lat + bands - 1, bands), lax.rem(lat + 1, bands)
    nfield, nrow, nlev, lon = fb.shape

    field_copies = {}
    wind_copies = {}
    for r in (0, 3, 1, 2):
        field_copies[r] = pltpu.make_async_copy(
            fields_hbm.at[:, :, r, :], fb.at[:, r], field_sem.at[r]
        )
        field_copies[r].start()
    for r in (1, 2, 0, 3):
        for i, src in enumerate((lon_hbm, lat_hbm, move_hbm)):
            wind_copies[i, r] = pltpu.make_async_copy(
                src.at[:, r, :], cb.at[i, r], wind_sem.at[i, r]
            )
            wind_copies[i, r].start()
    weight_copies = []
    moves = (
        (w1_hbm, w1),
        (b1_hbm, b1_line),
        (b2_hbm, b2_line),
        (b3_hbm, b3_line),
        (own_hbm, own_ref),
        (lent_hbm, lent_ref),
        (w2_hbm, w2),
        (w3_hbm, w3),
    )
    for i, (src, dst) in enumerate(moves):
        weight_copies.append(pltpu.make_async_copy(src, dst, weight_sem.at[i]))

    first_band = lat == 0
    last_band = lat == bands - 1
    late_owner = jnp.logical_and(first_band, lev == 0)
    late_peer = jnp.logical_and(first_band, lev != 0)

    barrier = pltpu.get_barrier_semaphore()

    @pl.when(jnp.logical_not(late_owner))
    def _():
        for off in ORDER:
            target = lax.rem(lev + off, count)
            pl.semaphore_signal(barrier, 1, device_id={"lev": target}, device_id_type=MESH)

    run = bands // 4
    place = lax.rem(lat, run)
    odd_south = jnp.logical_or(place == run - 1, late_owner)
    odd_north = jnp.logical_or(place == 0, jnp.logical_and(lat == 1, lev == 0))
    has_south = jnp.logical_not(last_band)
    has_north = jnp.logical_not(first_band)
    south_first = jnp.logical_and(has_south, odd_south)
    south_later = jnp.logical_and(has_south, jnp.logical_not(odd_south))
    north_first = jnp.logical_and(has_north, jnp.logical_not(odd_north))
    north_later = jnp.logical_and(has_north, odd_north)

    @pl.when(south_later)
    def _():
        pl.semaphore_signal(barrier, 1, device_id={"lat": south}, device_id_type=MESH)

    @pl.when(north_later)
    def _():
        pl.semaphore_signal(barrier, 1, device_id={"lat": north}, device_id_type=MESH)

    @pl.when(first_band)
    def _():
        halo_in[0] = jnp.zeros(halo_in.shape[1:], halo_in.dtype)

    @pl.when(last_band)
    def _():
        halo_in[1] = jnp.zeros(halo_in.shape[1:], halo_in.dtype)

    sub = lax.broadcasted_iota(jnp.int32, (nlev, lon), 0)

    def halo_tile(i, f, g):
        rows = slice((f % 2) * nlev, (f % 2 + 1) * nlev)
        tile = halo_in[i, g % 2, f // 2, :, (g // 2) * 128 : (g // 2 + 1) * 128]
        return tile.astype(jnp.float32)[rows]

    def moved(r, cols):
        last = jnp.logical_and(sub[:, cols] == nlev - 1, lev == count - 1)
        return jnp.where(last, 0.0, cb[2, r, :, cols])

    def advect(r, k):
        lonp = jnp.maximum(cb[0, r], 0.0)
        lonn = jnp.minimum(cb[0, r], 0.0)
        latp = jnp.maximum(cb[1, r], 0.0)
        latn = jnp.minimum(cb[1, r], 0.0)
        move = moved(r, slice(None))
        for f in range(nfield):
            x = fb[f, r]
            if r == nrow - 1:
                down = jnp.concatenate([halo_tile(1, f, g) for g in range(16)], axis=1)
            else:
                down = fb[f, r + 1]
            value = x - lonp * (x - pltpu.roll(x, 1, 1))
            value = value - lonn * (pltpu.roll(x, lon - 1, 1) - x)
            if r == 0:
                part[f, r] = value - latn * (down - x)
                continue
            value = value - latp * (x - fb[f, r - 1])
            value = value - latn * (down - x)
            flux = move * value
            turned = pltpu.roll(flux, 1, 0)
            part[f, r] = value - flux + jnp.where(sub == 0, 0.0, turned)
            flux_row[k * nfield + f : k * nfield + f + 1, :] = turned[0:1]

    def north_row(half):
        for g in range(half, 16, 2):
            cols = slice(g * 128, (g + 1) * 128)
            level = sub[:, cols]
            latp = jnp.maximum(cb[1, 0, :, cols], 0.0)
            move = moved(0, cols)
            edge = jnp.zeros((nlev, 128), jnp.float32)
            for pair in range(nfield // 2):
                values = []
                for f in (2 * pair, 2 * pair + 1):
                    x = fb[f, 0, :, cols]
                    value = part[f, 0, :, cols] - latp * (x - halo_tile(0, f, g))
                    flux = move * value
                    turned = pltpu.roll(flux, 1, 0)
                    values.append(value - flux + jnp.where(level == 0, 0.0, turned))
                    edge = jnp.where(level == f, pltpu.roll(flux, f + 1, 0), edge)
                both = jnp.concatenate(values, axis=0).astype(jnp.bfloat16)
                send[2][g, pair * 2 * nlev : (pair + 1) * 2 * nlev, :] = both
            flux_out[2][g] = edge[0:nfield].astype(jnp.bfloat16)

    def flux_copy(p, off):
        target = lax.rem(lev + off, count)
        return pltpu.make_async_remote_copy(
            src_ref=flux_out[p].at[target],
            dst_ref=flux_in[p].at[lev],
            send_sem=flux_send_sem.at[p, off - 1],
            recv_sem=flux_recv_sem.at[p, off - 1],
            device_id={"lev": target},
            device_id_type=MESH,
        )

    def halo_copy(i, half):
        return pltpu.make_async_remote_copy(
            src_ref=halo_out.at[i, half],
            dst_ref=halo_in.at[i, half],
            send_sem=halo_send_sem.at[i, half],
            recv_sem=halo_recv_sem.at[i, half],
            device_id={"lat": south if i == 0 else north},
            device_id_type=MESH,
        )

    def block_copy(p, off):
        target = lax.rem(lev + off, count)
        return pltpu.make_async_remote_copy(
            src_ref=send[p].at[target],
            dst_ref=recv[p].at[lev],
            send_sem=send_sem.at[p, off - 1],
            recv_sem=recv_sem.at[p, off - 1],
            device_id={"lev": target},
            device_id_type=MESH,
        )

    def finish(p):
        for i, r in enumerate(STAGES[p]):
            for pair in range(nfield // 2):
                both = jnp.concatenate([part[2 * pair, r], part[2 * pair + 1, r]], axis=0)
                both = both.astype(jnp.bfloat16)
                row = i * nfield * nlev + pair * 2 * nlev
                for g in range(16):
                    send[p][g, row : row + 2 * nlev, :] = both[:, g * 128 : (g + 1) * 128]
        edge = flux_row[0 : len(STAGES[p]) * nfield].astype(jnp.bfloat16)
        for g in range(16):
            flux_out[p][g] = edge[:, g * 128 : (g + 1) * 128]
        launch(p, (0, 1))

    def launch(p, halves):
        for off in ORDER:
            target = lax.rem(lev + off, count)
            if len(halves) == 1:
                wanted = lax.rem(target, 2) == halves[0]
            else:
                wanted = jnp.logical_not(jnp.logical_and(first_band, target == 0))

            @pl.when(wanted)
            def _():
                flux_copy(p, off).start()
                block_copy(p, off).start()

    field_copies[0].wait()
    field_copies[3].wait()
    for i, r in ((0, 3), (1, 0)):
        for pair in range(nfield // 2):
            both = jnp.concatenate([fb[2 * pair, r], fb[2 * pair + 1, r]], axis=0)
            both = both.astype(jnp.bfloat16)
            for g in range(16):
                halo_out[i, g % 2, pair, :, (g // 2) * 128 : (g // 2 + 1) * 128] = both[
                    :, g * 128 : (g + 1) * 128
                ]

    for copy in weight_copies:
        copy.start()

    def send_row(i, ready=None):
        if ready is not None:
            pl.semaphore_wait(ready, 1)
        for half in range(2):
            halo_copy(i, half).start()

    arrivals = count - 1 - late_peer.astype(jnp.int32)
    arrivals = arrivals + south_first.astype(jnp.int32) + north_first.astype(jnp.int32)
    pl.semaphore_wait(barrier, arrivals)

    @pl.when(south_first)
    def _():
        send_row(0)
        pl.semaphore_signal(ready_north, 1, device_id={"lat": south}, device_id_type=MESH)

    @pl.when(north_first)
    def _():
        send_row(1)
        pl.semaphore_signal(ready_south, 1, device_id={"lat": north}, device_id_type=MESH)

    @pl.when(late_owner)
    def _():
        for off in ORDER:
            target = lax.rem(lev + off, count)
            pl.semaphore_signal(ready_lev, 1, device_id={"lev": target}, device_id_type=MESH)

    field_copies[1].wait()
    field_copies[2].wait()
    for k, r in enumerate(STAGES[0]):
        for i in range(3):
            wind_copies[i, r].wait()
        advect(r, k)
    finish(0)

    for i in range(3):
        wind_copies[i, 0].wait()
    advect(0, 0)
    for copy in weight_copies:
        copy.wait()
    w1t[...] = w1[...].T
    w2t[...] = w2[...].T
    w3t[...] = w3[...].T
    for src, dst in ((b1_line, b1), (b2_line, b2), (b3_line, b3)):
        for i in range(dst.shape[0] // 128):
            line = jnp.broadcast_to(src[i * 128 : (i + 1) * 128][None], (128, 128))
            dst[i * 128 : (i + 1) * 128, :] = line.T

    @pl.when(south_later)
    def _():
        send_row(0, ready_south)

    for i in range(3):
        wind_copies[i, 3].wait()

    @pl.when(jnp.logical_not(last_band))
    def _():
        for half in range(2):
            halo_copy(1, half).wait_recv()

    advect(3, 0)
    finish(1)

    @pl.when(late_peer)
    def _():
        pl.semaphore_wait(ready_lev, 1)
        for p in range(2):
            flux_copy(p, count - lev).start()
            block_copy(p, count - lev).start()

    @pl.when(north_later)
    def _():
        send_row(1, ready_north)

    for half in range(2):

        @pl.when(jnp.logical_not(first_band))
        def _():
            halo_copy(0, half).wait_recv()

        north_row(half)
        launch(2, (half,))

    top = lax.broadcasted_iota(jnp.int32, (nlev, 128), 0) == 0

    def unpack(p):
        recv[p][lev] = send[p][lev]
        flux_in[p][lev] = flux_out[p][lev]
        for off in ORDER:
            flux_copy(p, off).wait_recv()
            block_copy(p, off).wait_recv()
        for i, r in enumerate(STAGES[p]):
            for pair in range(nfield // 2):
                pieces = ([], [])
                for g in range(16):
                    row = i * nfield * nlev + pair * 2 * nlev
                    both = recv[p][g, row : row + 2 * nlev].astype(jnp.float32)
                    for j in range(2):
                        piece = both[j * nlev : (j + 1) * nlev]
                        if g > 0:
                            k = i * nfield + 2 * pair + j
                            edge = flux_in[p][g - 1].astype(jnp.float32)[k : k + 1]
                            edge = jnp.broadcast_to(edge, (nlev, 128))
                            piece = piece + jnp.where(top, edge, 0.0)
                        pieces[j].append(piece)
                for j in range(2):
                    f = 2 * pair + j
                    whole = jnp.concatenate(pieces[j], axis=0)
                    ob[r, f * 128 : (f + 1) * 128] = whole
                    x_buf[f * 128 : (f + 1) * 128, i * 128 : (i + 1) * 128] = whole.astype(
                        jnp.bfloat16
                    )

    def physics(p):
        rows = STAGES[p]
        cols = 128 * len(rows)

        def wide(value):
            return jnp.concatenate([value] * len(rows), axis=1)

        x = x_buf[:, 0:cols]
        for start in range(0, 768, 256):
            span = slice(start, start + 256)
            v = jnp.dot(w1t[span], x, preferred_element_type=jnp.float32)
            h1[span, 0:cols] = silu(v + wide(b1[span])).astype(jnp.bfloat16)
        x = h1[:, 0:cols]
        for start in range(0, 640, 128):
            span = slice(start, start + 128)
            v = jnp.dot(w2t[span], x, preferred_element_type=jnp.float32)
            h2[span, 0:cols] = silu(v + wide(b2[span])).astype(jnp.bfloat16)
        x = h2[:, 0:cols]
        active = []
        for r in rows:
            hit = own_ref[0, 0, 0] == r
            for other in (own_ref[0, 0, 1], lent_ref[0, 0, 0], lent_ref[0, 0, 1]):
                hit = jnp.logical_or(hit, other == r)
            active.append(hit)
        for start in range(0, 512, 256):
            span = slice(start, start + 256)
            v = jnp.dot(w3t[span], x, preferred_element_type=jnp.float32)
            v = (v + wide(b3[span])).astype(jnp.bfloat16).astype(jnp.float32)
            for i, r in enumerate(rows):
                out[pl.ds(start * nrow + r, 256, stride=nrow), :] = ob[r, span] + jnp.where(
                    active[i], v[:, i * 128 : (i + 1) * 128], 0.0
                )

    for p in range(len(STAGES)):
        unpack(p)
        physics(p)

    @pl.when(jnp.logical_not(last_band))
    def _():
        for half in range(2):
            halo_copy(0, half).wait_send()

    @pl.when(jnp.logical_not(first_band))
    def _():
        for half in range(2):
            halo_copy(1, half).wait_send()

    for p in range(len(STAGES)):
        for off in ORDER:
            flux_copy(p, off).wait_send()
            block_copy(p, off).wait_send()


ORDER = (8, 7, 9, 6, 10, 5, 11, 4, 12, 3, 13, 2, 14, 1, 15)


def in_hbm(value):
    return pltpu.with_memory_space_constraint(value, pltpu.HBM)


def body(
    fields,
    courant_lon,
    courant_lat,
    displacement,
    own_slot,
    lent_slot,
    w_first,
    bias_first,
    w_second,
    bias_second,
    w_third,
    bias_third,
):
    nfield, nlev, nrow, lon = fields.shape
    count = lax.axis_size("lev")
    width = nfield * nlev * count
    part = lon // count
    hidden = (w_first.shape[1], w_second.shape[1])
    f32, bf16 = jnp.float32, jnp.bfloat16
    hbm = pl.BlockSpec(memory_space=pltpu.HBM)
    dma = pltpu.SemaphoreType.DMA
    stages = len(STAGES)
    buffers = []
    for rows in STAGES:
        buffers += [pltpu.VMEM((count, len(rows) * nfield, part), bf16)] * 2
        buffers += [pltpu.VMEM((count, len(rows) * nfield * nlev, part), bf16)] * 2
    return pl.pallas_call(
        kernel,
        name="tracer",
        out_shape=jax.ShapeDtypeStruct((width * nrow, part), f32),
        in_specs=[hbm] * 12,
        out_specs=pl.BlockSpec(memory_space=pltpu.VMEM),
        scratch_shapes=[
            pltpu.VMEM((nfield, nrow, nlev, lon), f32),
            pltpu.VMEM((3, nrow, nlev, lon), f32),
            pltpu.VMEM((nfield, nrow, nlev, lon), f32),
            pltpu.VMEM((2, 2, nfield // 2, 2 * nlev, lon // 2), bf16),
            pltpu.VMEM((2, 2, nfield // 2, 2 * nlev, lon // 2), bf16),
            pltpu.VMEM((2 * nfield, lon), f32),
            *buffers,
            pltpu.VMEM((width, hidden[0]), bf16),
            pltpu.VMEM((hidden[0], hidden[1]), bf16),
            pltpu.VMEM((hidden[1], width), bf16),
            pltpu.VMEM((hidden[0], width), bf16),
            pltpu.VMEM((hidden[1], hidden[0]), bf16),
            pltpu.VMEM((width, hidden[1]), bf16),
            pltpu.VMEM((hidden[0], 128), f32),
            pltpu.VMEM((hidden[1], 128), f32),
            pltpu.VMEM((width, 128), f32),
            pltpu.VMEM((nrow, width, part), f32),
            pltpu.VMEM((width, 2 * part), bf16),
            pltpu.VMEM((hidden[0], 2 * part), bf16),
            pltpu.VMEM((hidden[1], 2 * part), bf16),
            pltpu.SMEM(own_slot.shape, jnp.int32),
            pltpu.SMEM(lent_slot.shape, jnp.int32),
            pltpu.VMEM(bias_first.shape, f32),
            pltpu.VMEM(bias_second.shape, f32),
            pltpu.VMEM(bias_third.shape, f32),
            dma((nrow,)),
            dma((3, nrow)),
            dma((8,)),
            dma((2, 2)),
            dma((2, 2)),
            pltpu.SemaphoreType.REGULAR,
            pltpu.SemaphoreType.REGULAR,
            pltpu.SemaphoreType.REGULAR,
            dma((stages, count - 1)),
            dma((stages, count - 1)),
            dma((stages, count - 1)),
            dma((stages, count - 1)),
        ],
        compiler_params=pltpu.CompilerParams(
            collective_id=0, has_side_effects=True, vmem_limit_bytes=48 << 20
        ),
    )(
        in_hbm(fields),
        in_hbm(courant_lon),
        in_hbm(courant_lat),
        in_hbm(displacement),
        in_hbm(own_slot),
        in_hbm(lent_slot),
        in_hbm(w_first),
        in_hbm(bias_first),
        in_hbm(w_second),
        in_hbm(bias_second),
        in_hbm(w_third),
        in_hbm(bias_third),
    ).reshape(width, nrow, part)


def solution(mesh):
    in_specs = (
        P(None, "lev", "lat", None),
        P("lev", "lat", None),
        P("lev", "lat", None),
        P("lev", "lat", None),
        P("lev", "lat", None),
        P("lev", "lat", None),
        P(),
        P(),
        P(),
        P(),
        P(),
        P(),
    )
    out_specs = P(None, "lat", "lev")
    return jax.shard_map(body, mesh=mesh, in_specs=in_specs, out_specs=out_specs, check_vma=False)
```

```python
import jax
import jax.numpy as jnp
from jax import lax
from jax.experimental import pallas as pl
from jax.experimental.pallas import tpu as pltpu
from jax.sharding import PartitionSpec as P

MESH = pl.DeviceIdType.MESH
STAGES = ((1, 2), (3,), (0,))


def silu(value):
    return value * (0.5 + 0.5 * jnp.tanh(0.5 * value))


def kernel(
    fields_hbm,
    lon_hbm,
    lat_hbm,
    move_hbm,
    own_hbm,
    lent_hbm,
    w1_hbm,
    b1_hbm,
    w2_hbm,
    b2_hbm,
    w3_hbm,
    b3_hbm,
    out,
    fb,
    cb,
    part,
    halo_out,
    halo_in,
    flux_row,
    *refs,
):
    buffers, refs = refs[: 4 * len(STAGES)], refs[4 * len(STAGES) :]
    flux_out, flux_in, send, recv = (buffers[k :: 4] for k in range(4))
    (
        w1,
        w2,
        w3,
        w1t,
        w2t,
        w3t,
        b1,
        b2,
        b3,
        ob,
        x_buf,
        h1,
        h2,
        own_ref,
        lent_ref,
        b1_line,
        b2_line,
        b3_line,
        field_sem,
        wind_sem,
        weight_sem,
        halo_send_sem,
        halo_recv_sem,
        ready_north,
        ready_south,
        ready_lev,
        flux_send_sem,
        flux_recv_sem,
        send_sem,
        recv_sem,
    ) = refs
    count = lax.axis_size("lev")
    bands = lax.axis_size("lat")
    lev = lax.axis_index("lev")
    lat = lax.axis_index("lat")
    north, south = lax.rem(lat + bands - 1, bands), lax.rem(lat + 1, bands)
    nfield, nrow, nlev, lon = fb.shape

    first_band = lat == 0
    last_band = lat == bands - 1
    late_owner = jnp.logical_and(first_band, lev == 0)
    late_peer = jnp.logical_and(first_band, lev != 0)

    barrier = pltpu.get_barrier_semaphore()

    @pl.when(jnp.logical_not(late_owner))
    def _():
        for off in ORDER:
            target = lax.rem(lev + off, count)
            pl.semaphore_signal(barrier, 1, device_id={"lev": target}, device_id_type=MESH)

    run = bands // 4
    place = lax.rem(lat, run)
    odd_south = jnp.logical_or(place == run - 1, late_owner)
    odd_north = jnp.logical_or(place == 0, jnp.logical_and(lat == 1, lev == 0))
    has_south = jnp.logical_not(last_band)
    has_north = jnp.logical_not(first_band)
    south_first = jnp.logical_and(has_south, odd_south)
    south_later = jnp.logical_and(has_south, jnp.logical_not(odd_south))
    north_first = jnp.logical_and(has_north, jnp.logical_not(odd_north))
    north_later = jnp.logical_and(has_north, odd_north)

    @pl.when(south_later)
    def _():
        pl.semaphore_signal(barrier, 1, device_id={"lat": south}, device_id_type=MESH)

    @pl.when(north_later)
    def _():
        pl.semaphore_signal(barrier, 1, device_id={"lat": north}, device_id_type=MESH)

    field_copies = {}
    wind_copies = {}
    for r in (0, 3, 1, 2):
        field_copies[r] = pltpu.make_async_copy(
            fields_hbm.at[:, :, r, :], fb.at[:, r], field_sem.at[r]
        )
        field_copies[r].start()
    for r in (1, 2, 0, 3):
        for i, src in enumerate((lon_hbm, lat_hbm, move_hbm)):
            wind_copies[i, r] = pltpu.make_async_copy(
                src.at[:, r, :], cb.at[i, r], wind_sem.at[r]
            )
            wind_copies[i, r].start()
    weight_copies = []
    moves = (
        (w1_hbm, w1),
        (b1_hbm, b1_line),
        (b2_hbm, b2_line),
        (b3_hbm, b3_line),
        (own_hbm, own_ref),
        (lent_hbm, lent_ref),
        (w2_hbm, w2),
        (w3_hbm, w3),
    )
    for i, (src, dst) in enumerate(moves):
        weight_copies.append(pltpu.make_async_copy(src, dst, weight_sem.at[i]))

    @pl.when(first_band)
    def _():
        halo_in[0] = jnp.zeros(halo_in.shape[1:], halo_in.dtype)

    @pl.when(last_band)
    def _():
        halo_in[1] = jnp.zeros(halo_in.shape[1:], halo_in.dtype)

    sub = lax.broadcasted_iota(jnp.int32, (nlev, lon), 0)

    def halo_tile(i, f, g):
        rows = slice((f % 2) * nlev, (f % 2 + 1) * nlev)
        tile = halo_in[i, g % 2, f // 2, :, (g // 2) * 128 : (g // 2 + 1) * 128]
        return tile.astype(jnp.float32)[rows]

    def moved(r, cols):
        last = jnp.logical_and(sub[:, cols] == nlev - 1, lev == count - 1)
        return jnp.where(last, 0.0, cb[2, r, :, cols])

    def advect(r, k):
        lonp = jnp.maximum(cb[0, r], 0.0)
        lonn = jnp.minimum(cb[0, r], 0.0)
        latp = jnp.maximum(cb[1, r], 0.0)
        latn = jnp.minimum(cb[1, r], 0.0)
        move = moved(r, slice(None))
        for f in range(nfield):
            x = fb[f, r]
            if r == nrow - 1:
                down = jnp.concatenate([halo_tile(1, f, g) for g in range(16)], axis=1)
            else:
                down = fb[f, r + 1]
            value = x - lonp * (x - pltpu.roll(x, 1, 1))
            value = value - lonn * (pltpu.roll(x, lon - 1, 1) - x)
            if r == 0:
                part[f, r] = value - latn * (down - x)
                continue
            value = value - latp * (x - fb[f, r - 1])
            value = value - latn * (down - x)
            flux = move * value
            turned = pltpu.roll(flux, 1, 0)
            part[f, r] = value - flux + jnp.where(sub == 0, 0.0, turned)
            flux_row[k * nfield + f : k * nfield + f + 1, :] = turned[0:1]

    def north_row(half):
        for g in range(half, 16, 2):
            cols = slice(g * 128, (g + 1) * 128)
            level = sub[:, cols]
            latp = jnp.maximum(cb[1, 0, :, cols], 0.0)
            move = moved(0, cols)
            edge = jnp.zeros((nlev, 128), jnp.float32)
            for pair in range(nfield // 2):
                values = []
                for f in (2 * pair, 2 * pair + 1):
                    x = fb[f, 0, :, cols]
                    value = part[f, 0, :, cols] - latp * (x - halo_tile(0, f, g))
                    flux = move * value
                    turned = pltpu.roll(flux, 1, 0)
                    values.append(value - flux + jnp.where(level == 0, 0.0, turned))
                    edge = jnp.where(level == f, pltpu.roll(flux, f + 1, 0), edge)
                both = jnp.concatenate(values, axis=0).astype(jnp.bfloat16)
                send[2][g, pair * 2 * nlev : (pair + 1) * 2 * nlev, :] = both
            flux_out[2][g] = edge[0:nfield].astype(jnp.bfloat16)

    def flux_copy(p, off):
        target = lax.rem(lev + off, count)
        return pltpu.make_async_remote_copy(
            src_ref=flux_out[p].at[target],
            dst_ref=flux_in[p].at[lev],
            send_sem=flux_send_sem.at[p],
            recv_sem=flux_recv_sem.at[p],
            device_id={"lev": target},
            device_id_type=MESH,
        )

    def halo_copy(i, half):
        return pltpu.make_async_remote_copy(
            src_ref=halo_out.at[i, half],
            dst_ref=halo_in.at[i, half],
            send_sem=halo_send_sem.at[i, half],
            recv_sem=halo_recv_sem.at[i, half],
            device_id={"lat": south if i == 0 else north},
            device_id_type=MESH,
        )

    def block_copy(p, off):
        target = lax.rem(lev + off, count)
        return pltpu.make_async_remote_copy(
            src_ref=send[p].at[target],
            dst_ref=recv[p].at[lev],
            send_sem=send_sem.at[p],
            recv_sem=recv_sem.at[p],
            device_id={"lev": target},
            device_id_type=MESH,
        )

    def await_winds(r):
        row = cb.at[:, r]
        pltpu.make_async_copy(row, row, wind_sem.at[r]).wait()

    def await_all(ref, sem):
        rows = ref.at[pl.ds(0, count - 1)]
        pltpu.make_async_copy(rows, rows, sem).wait()

    def finish(p):
        for i, r in enumerate(STAGES[p]):
            for pair in range(nfield // 2):
                both = jnp.concatenate([part[2 * pair, r], part[2 * pair + 1, r]], axis=0)
                both = both.astype(jnp.bfloat16)
                row = i * nfield * nlev + pair * 2 * nlev
                for g in range(16):
                    send[p][g, row : row + 2 * nlev, :] = both[:, g * 128 : (g + 1) * 128]
        edge = flux_row[0 : len(STAGES[p]) * nfield].astype(jnp.bfloat16)
        for g in range(16):
            flux_out[p][g] = edge[:, g * 128 : (g + 1) * 128]
        launch(p, (0, 1))

    def launch(p, halves):
        for off in ORDER:
            target = lax.rem(lev + off, count)
            if len(halves) == 1:
                wanted = lax.rem(target, 2) == halves[0]
            else:
                wanted = jnp.logical_not(jnp.logical_and(first_band, target == 0))

            @pl.when(wanted)
            def _():
                flux_copy(p, off).start()
                block_copy(p, off).start()

    field_copies[0].wait()
    field_copies[3].wait()
    for i, r in ((0, 3), (1, 0)):
        for pair in range(nfield // 2):
            both = jnp.concatenate([fb[2 * pair, r], fb[2 * pair + 1, r]], axis=0)
            both = both.astype(jnp.bfloat16)
            for g in range(16):
                halo_out[i, g % 2, pair, :, (g // 2) * 128 : (g // 2 + 1) * 128] = both[
                    :, g * 128 : (g + 1) * 128
                ]

    for copy in weight_copies:
        copy.start()

    def send_row(i, ready=None):
        if ready is not None:
            pl.semaphore_wait(ready, 1)
        for half in range(2):
            halo_copy(i, half).start()

    arrivals = count - 1 - late_peer.astype(jnp.int32)
    arrivals = arrivals + south_first.astype(jnp.int32) + north_first.astype(jnp.int32)
    pl.semaphore_wait(barrier, arrivals)

    @pl.when(south_first)
    def _():
        send_row(0)
        pl.semaphore_signal(ready_north, 1, device_id={"lat": south}, device_id_type=MESH)

    @pl.when(north_first)
    def _():
        send_row(1)
        pl.semaphore_signal(ready_south, 1, device_id={"lat": north}, device_id_type=MESH)

    @pl.when(late_owner)
    def _():
        for off in ORDER:
            target = lax.rem(lev + off, count)
            pl.semaphore_signal(ready_lev, 1, device_id={"lev": target}, device_id_type=MESH)

    field_copies[1].wait()
    field_copies[2].wait()
    for k, r in enumerate(STAGES[0]):
        await_winds(r)
        advect(r, k)
    finish(0)

    await_winds(0)
    advect(0, 0)
    for copy in weight_copies:
        copy.wait()
    w1t[...] = w1[...].T
    w2t[...] = w2[...].T
    w3t[...] = w3[...].T
    for src, dst in ((b1_line, b1), (b2_line, b2), (b3_line, b3)):
        for i in range(dst.shape[0] // 128):
            line = jnp.broadcast_to(src[i * 128 : (i + 1) * 128][None], (128, 128))
            dst[i * 128 : (i + 1) * 128, :] = line.T

    @pl.when(south_later)
    def _():
        send_row(0, ready_south)

    await_winds(3)

    @pl.when(jnp.logical_not(last_band))
    def _():
        for half in range(2):
            halo_copy(1, half).wait_recv()

    advect(3, 0)
    finish(1)

    @pl.when(late_peer)
    def _():
        pl.semaphore_wait(ready_lev, 1)
        for p in range(2):
            flux_copy(p, count - lev).start()
            block_copy(p, count - lev).start()

    @pl.when(north_later)
    def _():
        send_row(1, ready_north)

    for half in range(2):

        @pl.when(jnp.logical_not(first_band))
        def _():
            halo_copy(0, half).wait_recv()

        north_row(half)
        launch(2, (half,))

    def drain():
        @pl.when(has_south)
        def _():
            for half in range(2):
                halo_copy(0, half).wait_send()

        @pl.when(has_north)
        def _():
            for half in range(2):
                halo_copy(1, half).wait_send()

        for p in range(len(STAGES)):
            await_all(flux_out[p], flux_send_sem.at[p])
            await_all(send[p], send_sem.at[p])

    top = lax.broadcasted_iota(jnp.int32, (nlev, 128), 0) == 0

    def unpack(p):
        await_all(flux_in[p], flux_recv_sem.at[p])
        await_all(recv[p], recv_sem.at[p])
        recv[p][lev] = send[p][lev]
        flux_in[p][lev] = flux_out[p][lev]
        for i, r in enumerate(STAGES[p]):
            for pair in range(nfield // 2):
                pieces = ([], [])
                for g in range(16):
                    row = i * nfield * nlev + pair * 2 * nlev
                    both = recv[p][g, row : row + 2 * nlev].astype(jnp.float32)
                    for j in range(2):
                        piece = both[j * nlev : (j + 1) * nlev]
                        if g > 0:
                            k = i * nfield + 2 * pair + j
                            edge = flux_in[p][g - 1].astype(jnp.float32)[k : k + 1]
                            edge = jnp.broadcast_to(edge, (nlev, 128))
                            piece = piece + jnp.where(top, edge, 0.0)
                        pieces[j].append(piece)
                for j in range(2):
                    f = 2 * pair + j
                    whole = jnp.concatenate(pieces[j], axis=0)
                    ob[r, f * 128 : (f + 1) * 128] = whole
                    x_buf[f * 128 : (f + 1) * 128, i * 128 : (i + 1) * 128] = whole.astype(
                        jnp.bfloat16
                    )

    def physics(p):
        rows = STAGES[p]
        cols = 128 * len(rows)

        def wide(value):
            return jnp.concatenate([value] * len(rows), axis=1)

        x = x_buf[:, 0:cols]
        for start in range(0, 768, 256):
            span = slice(start, start + 256)
            v = jnp.dot(w1t[span], x, preferred_element_type=jnp.float32)
            h1[span, 0:cols] = silu(v + wide(b1[span])).astype(jnp.bfloat16)
        x = h1[:, 0:cols]
        for start in range(0, 640, 128):
            span = slice(start, start + 128)
            v = jnp.dot(w2t[span], x, preferred_element_type=jnp.float32)
            h2[span, 0:cols] = silu(v + wide(b2[span])).astype(jnp.bfloat16)
        x = h2[:, 0:cols]
        active = []
        for r in rows:
            hit = own_ref[0, 0, 0] == r
            for other in (own_ref[0, 0, 1], lent_ref[0, 0, 0], lent_ref[0, 0, 1]):
                hit = jnp.logical_or(hit, other == r)
            active.append(hit)
        for start in range(0, 512, 256):
            span = slice(start, start + 256)
            v = jnp.dot(w3t[span], x, preferred_element_type=jnp.float32)
            v = (v + wide(b3[span])).astype(jnp.bfloat16).astype(jnp.float32)
            for i, r in enumerate(rows):
                out[pl.ds(start * nrow + r, 256, stride=nrow), :] = ob[r, span] + jnp.where(
                    active[i], v[:, i * 128 : (i + 1) * 128], 0.0
                )

    for p in range(len(STAGES)):
        if p == len(STAGES) - 1:
            drain()
        unpack(p)
        physics(p)


ORDER = (8, 7, 9, 6, 10, 5, 11, 4, 12, 3, 13, 2, 14, 1, 15)


def in_hbm(value):
    return pltpu.with_memory_space_constraint(value, pltpu.HBM)


def body(
    fields,
    courant_lon,
    courant_lat,
    displacement,
    own_slot,
    lent_slot,
    w_first,
    bias_first,
    w_second,
    bias_second,
    w_third,
    bias_third,
):
    nfield, nlev, nrow, lon = fields.shape
    count = lax.axis_size("lev")
    width = nfield * nlev * count
    part = lon // count
    hidden = (w_first.shape[1], w_second.shape[1])
    f32, bf16 = jnp.float32, jnp.bfloat16
    hbm = pl.BlockSpec(memory_space=pltpu.HBM)
    dma = pltpu.SemaphoreType.DMA
    stages = len(STAGES)
    buffers = []
    for rows in STAGES:
        buffers += [pltpu.VMEM((count, len(rows) * nfield, part), bf16)] * 2
        buffers += [pltpu.VMEM((count, len(rows) * nfield * nlev, part), bf16)] * 2
    return pl.pallas_call(
        kernel,
        name="tracer",
        out_shape=jax.ShapeDtypeStruct((width * nrow, part), f32),
        in_specs=[hbm] * 12,
        out_specs=pl.BlockSpec(memory_space=pltpu.VMEM),
        scratch_shapes=[
            pltpu.VMEM((nfield, nrow, nlev, lon), f32),
            pltpu.VMEM((3, nrow, nlev, lon), f32),
            pltpu.VMEM((nfield, nrow, nlev, lon), f32),
            pltpu.VMEM((2, 2, nfield // 2, 2 * nlev, lon // 2), bf16),
            pltpu.VMEM((2, 2, nfield // 2, 2 * nlev, lon // 2), bf16),
            pltpu.VMEM((2 * nfield, lon), f32),
            *buffers,
            pltpu.VMEM((width, hidden[0]), bf16),
            pltpu.VMEM((hidden[0], hidden[1]), bf16),
            pltpu.VMEM((hidden[1], width), bf16),
            pltpu.VMEM((hidden[0], width), bf16),
            pltpu.VMEM((hidden[1], hidden[0]), bf16),
            pltpu.VMEM((width, hidden[1]), bf16),
            pltpu.VMEM((hidden[0], 128), f32),
            pltpu.VMEM((hidden[1], 128), f32),
            pltpu.VMEM((width, 128), f32),
            pltpu.VMEM((nrow, width, part), f32),
            pltpu.VMEM((width, 2 * part), bf16),
            pltpu.VMEM((hidden[0], 2 * part), bf16),
            pltpu.VMEM((hidden[1], 2 * part), bf16),
            pltpu.SMEM(own_slot.shape, jnp.int32),
            pltpu.SMEM(lent_slot.shape, jnp.int32),
            pltpu.VMEM(bias_first.shape, f32),
            pltpu.VMEM(bias_second.shape, f32),
            pltpu.VMEM(bias_third.shape, f32),
            dma((nrow,)),
            dma((nrow,)),
            dma((8,)),
            dma((2, 2)),
            dma((2, 2)),
            pltpu.SemaphoreType.REGULAR,
            pltpu.SemaphoreType.REGULAR,
            pltpu.SemaphoreType.REGULAR,
            dma((stages,)),
            dma((stages,)),
            dma((stages,)),
            dma((stages,)),
        ],
        compiler_params=pltpu.CompilerParams(
            collective_id=0, has_side_effects=True, vmem_limit_bytes=48 << 20
        ),
    )(
        in_hbm(fields),
        in_hbm(courant_lon),
        in_hbm(courant_lat),
        in_hbm(displacement),
        in_hbm(own_slot),
        in_hbm(lent_slot),
        in_hbm(w_first),
        in_hbm(bias_first),
        in_hbm(w_second),
        in_hbm(bias_second),
        in_hbm(w_third),
        in_hbm(bias_third),
    ).reshape(width, nrow, part)


def solution(mesh):
    in_specs = (
        P(None, "lev", "lat", None),
        P("lev", "lat", None),
        P("lev", "lat", None),
        P("lev", "lat", None),
        P("lev", "lat", None),
        P("lev", "lat", None),
        P(),
        P(),
        P(),
        P(),
        P(),
        P(),
    )
    out_specs = P(None, "lat", "lev")
    return jax.shard_map(body, mesh=mesh, in_specs=in_specs, out_specs=out_specs, check_vma=False)
```

```python
import jax
import jax.numpy as jnp
from jax import lax
from jax.experimental import pallas as pl
from jax.experimental.pallas import tpu as pltpu
from jax.sharding import PartitionSpec as P

MESH = pl.DeviceIdType.MESH
STAGES = ((1, 2), (3,), (0,))


def silu(value):
    return value * (0.5 + 0.5 * jnp.tanh(0.5 * value))


def kernel(
    fields_hbm,
    lon_hbm,
    lat_hbm,
    move_hbm,
    own_hbm,
    lent_hbm,
    w1_hbm,
    b1_hbm,
    w2_hbm,
    b2_hbm,
    w3_hbm,
    b3_hbm,
    out,
    fb,
    cb,
    part,
    halo_out,
    halo_in,
    flux_row,
    *refs,
):
    buffers, refs = refs[: 4 * len(STAGES)], refs[4 * len(STAGES) :]
    flux_out, flux_in, send, recv = (buffers[k :: 4] for k in range(4))
    (
        w1,
        w2,
        w3,
        w1t,
        w2t,
        w3t,
        b1,
        b2,
        b3,
        ob,
        x_buf,
        h1,
        h2,
        own_ref,
        lent_ref,
        b1_line,
        b2_line,
        b3_line,
        field_sem,
        wind_sem,
        weight_sem,
        halo_send_sem,
        halo_recv_sem,
        ring_count,
        ring_ready,
        ready_north,
        ready_south,
        ready_lev,
        flux_send_sem,
        flux_recv_sem,
        send_sem,
        recv_sem,
    ) = refs
    count = lax.axis_size("lev")
    bands = lax.axis_size("lat")
    lev = lax.axis_index("lev")
    lat = lax.axis_index("lat")
    north, south = lax.rem(lat + bands - 1, bands), lax.rem(lat + 1, bands)
    nfield, nrow, nlev, lon = fb.shape

    first_band = lat == 0
    last_band = lat == bands - 1
    late_owner = jnp.logical_and(first_band, lev == 0)
    late_peer = jnp.logical_and(first_band, lev != 0)

    barrier = pltpu.get_barrier_semaphore()

    run = bands // 4
    place = lax.rem(lat, run)
    has_south = jnp.logical_not(last_band)
    has_north = jnp.logical_not(first_band)
    told = jnp.logical_and(place == run - 1, has_south)
    teller = jnp.logical_and(place == 0, has_north)

    @pl.when(jnp.logical_not(jnp.logical_or(late_owner, told)))
    def _():
        for off in ORDER:
            target = lax.rem(lev + off, count)
            pl.semaphore_signal(barrier, 1, device_id={"lev": target}, device_id_type=MESH)

    odd_south = jnp.logical_or(place == run - 1, late_owner)
    odd_north = jnp.logical_or(place == 0, jnp.logical_and(lat == 1, lev == 0))
    south_first = jnp.logical_and(has_south, odd_south)
    south_later = jnp.logical_and(has_south, jnp.logical_not(odd_south))
    north_first = jnp.logical_and(has_north, jnp.logical_not(odd_north))
    north_later = jnp.logical_and(has_north, odd_north)

    @pl.when(south_later)
    def _():
        pl.semaphore_signal(barrier, 1, device_id={"lat": south}, device_id_type=MESH)

    @pl.when(north_later)
    def _():
        pl.semaphore_signal(barrier, 1, device_id={"lat": north}, device_id_type=MESH)

    field_copies = {}
    wind_copies = {}
    for r in (0, 3, 1, 2):
        field_copies[r] = pltpu.make_async_copy(
            fields_hbm.at[:, :, r, :], fb.at[:, r], field_sem.at[r]
        )
        field_copies[r].start()
    for r in (1, 2, 0, 3):
        for i, src in enumerate((lon_hbm, lat_hbm, move_hbm)):
            wind_copies[i, r] = pltpu.make_async_copy(
                src.at[:, r, :], cb.at[i, r], wind_sem.at[r]
            )
            wind_copies[i, r].start()
    weight_copies = []
    moves = (
        (w1_hbm, w1),
        (b1_hbm, b1_line),
        (b2_hbm, b2_line),
        (b3_hbm, b3_line),
        (own_hbm, own_ref),
        (lent_hbm, lent_ref),
        (w2_hbm, w2),
        (w3_hbm, w3),
    )
    for i, (src, dst) in enumerate(moves):
        weight_copies.append(pltpu.make_async_copy(src, dst, weight_sem.at[i]))

    @pl.when(first_band)
    def _():
        halo_in[0] = jnp.zeros(halo_in.shape[1:], halo_in.dtype)

    @pl.when(last_band)
    def _():
        halo_in[1] = jnp.zeros(halo_in.shape[1:], halo_in.dtype)

    sub = lax.broadcasted_iota(jnp.int32, (nlev, lon), 0)

    def halo_tile(i, f, g):
        rows = slice((f % 2) * nlev, (f % 2 + 1) * nlev)
        tile = halo_in[i, g % 2, f // 2, :, (g // 2) * 128 : (g // 2 + 1) * 128]
        return tile.astype(jnp.float32)[rows]

    def moved(r, cols):
        last = jnp.logical_and(sub[:, cols] == nlev - 1, lev == count - 1)
        return jnp.where(last, 0.0, cb[2, r, :, cols])

    def advect(r, k):
        lonp = jnp.maximum(cb[0, r], 0.0)
        lonn = jnp.minimum(cb[0, r], 0.0)
        latp = jnp.maximum(cb[1, r], 0.0)
        latn = jnp.minimum(cb[1, r], 0.0)
        move = moved(r, slice(None))
        for f in range(nfield):
            x = fb[f, r]
            if r == nrow - 1:
                down = jnp.concatenate([halo_tile(1, f, g) for g in range(16)], axis=1)
            else:
                down = fb[f, r + 1]
            value = x - lonp * (x - pltpu.roll(x, 1, 1))
            value = value - lonn * (pltpu.roll(x, lon - 1, 1) - x)
            if r == 0:
                part[f, r] = value - latn * (down - x)
                continue
            value = value - latp * (x - fb[f, r - 1])
            value = value - latn * (down - x)
            flux = move * value
            turned = pltpu.roll(flux, 1, 0)
            part[f, r] = value - flux + jnp.where(sub == 0, 0.0, turned)
            flux_row[k * nfield + f : k * nfield + f + 1, :] = turned[0:1]

    def north_row(half):
        for g in range(half, 16, 2):
            cols = slice(g * 128, (g + 1) * 128)
            level = sub[:, cols]
            latp = jnp.maximum(cb[1, 0, :, cols], 0.0)
            move = moved(0, cols)
            edge = jnp.zeros((nlev, 128), jnp.float32)
            for pair in range(nfield // 2):
                values = []
                for f in (2 * pair, 2 * pair + 1):
                    x = fb[f, 0, :, cols]
                    value = part[f, 0, :, cols] - latp * (x - halo_tile(0, f, g))
                    flux = move * value
                    turned = pltpu.roll(flux, 1, 0)
                    values.append(value - flux + jnp.where(level == 0, 0.0, turned))
                    edge = jnp.where(level == f, pltpu.roll(flux, f + 1, 0), edge)
                both = jnp.concatenate(values, axis=0).astype(jnp.bfloat16)
                send[2][g, pair * 2 * nlev : (pair + 1) * 2 * nlev, :] = both
            flux_out[2][g] = edge[0:nfield].astype(jnp.bfloat16)

    def flux_copy(p, off):
        target = lax.rem(lev + off, count)
        return pltpu.make_async_remote_copy(
            src_ref=flux_out[p].at[target],
            dst_ref=flux_in[p].at[lev],
            send_sem=flux_send_sem.at[p],
            recv_sem=flux_recv_sem.at[p],
            device_id={"lev": target},
            device_id_type=MESH,
        )

    def halo_copy(i, half):
        return pltpu.make_async_remote_copy(
            src_ref=halo_out.at[i, half],
            dst_ref=halo_in.at[i, half],
            send_sem=halo_send_sem.at[i, half],
            recv_sem=halo_recv_sem.at[i, half],
            device_id={"lat": south if i == 0 else north},
            device_id_type=MESH,
        )

    def block_copy(p, off):
        target = lax.rem(lev + off, count)
        return pltpu.make_async_remote_copy(
            src_ref=send[p].at[target],
            dst_ref=recv[p].at[lev],
            send_sem=send_sem.at[p],
            recv_sem=recv_sem.at[p],
            device_id={"lev": target},
            device_id_type=MESH,
        )

    def await_winds(r):
        row = cb.at[:, r]
        pltpu.make_async_copy(row, row, wind_sem.at[r]).wait()

    def await_all(ref, sem):
        rows = ref.at[pl.ds(0, count - 1)]
        pltpu.make_async_copy(rows, rows, sem).wait()

    def finish(p):
        for i, r in enumerate(STAGES[p]):
            for pair in range(nfield // 2):
                both = jnp.concatenate([part[2 * pair, r], part[2 * pair + 1, r]], axis=0)
                both = both.astype(jnp.bfloat16)
                row = i * nfield * nlev + pair * 2 * nlev
                for g in range(16):
                    send[p][g, row : row + 2 * nlev, :] = both[:, g * 128 : (g + 1) * 128]
        edge = flux_row[0 : len(STAGES[p]) * nfield].astype(jnp.bfloat16)
        for g in range(16):
            flux_out[p][g] = edge[:, g * 128 : (g + 1) * 128]
        if p == 0:

            @pl.when(told)
            def _():
                pl.semaphore_wait(ring_ready, 1)

        launch(p, (0, 1))

    def launch(p, halves):
        for off in ORDER:
            target = lax.rem(lev + off, count)
            if len(halves) == 1:
                wanted = lax.rem(target, 2) == halves[0]
            else:
                wanted = jnp.logical_not(jnp.logical_and(first_band, target == 0))

            @pl.when(wanted)
            def _():
                flux_copy(p, off).start()
                block_copy(p, off).start()

    field_copies[0].wait()
    field_copies[3].wait()
    for i, r in ((0, 3), (1, 0)):
        for pair in range(nfield // 2):
            both = jnp.concatenate([fb[2 * pair, r], fb[2 * pair + 1, r]], axis=0)
            both = both.astype(jnp.bfloat16)
            for g in range(16):
                halo_out[i, g % 2, pair, :, (g // 2) * 128 : (g // 2 + 1) * 128] = both[
                    :, g * 128 : (g + 1) * 128
                ]

    for copy in weight_copies:
        copy.start()

    def send_row(i, ready=None):
        if ready is not None:
            pl.semaphore_wait(ready, 1)
        for half in range(2):
            halo_copy(i, half).start()

    arrivals = (count - 1) * (1 - told.astype(jnp.int32)) - late_peer.astype(jnp.int32)
    arrivals = arrivals + south_first.astype(jnp.int32) + north_first.astype(jnp.int32)
    pl.semaphore_wait(barrier, arrivals)

    @pl.when(south_first)
    def _():
        send_row(0)
        pl.semaphore_signal(ready_north, 1, device_id={"lat": south}, device_id_type=MESH)

    @pl.when(north_first)
    def _():
        send_row(1)
        pl.semaphore_signal(ready_south, 1, device_id={"lat": north}, device_id_type=MESH)

    @pl.when(late_owner)
    def _():
        for off in ORDER:
            target = lax.rem(lev + off, count)
            pl.semaphore_signal(ready_lev, 1, device_id={"lev": target}, device_id_type=MESH)

    field_copies[1].wait()
    field_copies[2].wait()
    for k, r in enumerate(STAGES[0]):
        await_winds(r)
        advect(r, k)
    finish(0)

    await_winds(0)
    advect(0, 0)
    for copy in weight_copies:
        copy.wait()
    w1t[...] = w1[...].T
    w2t[...] = w2[...].T
    w3t[...] = w3[...].T
    for src, dst in ((b1_line, b1), (b2_line, b2), (b3_line, b3)):
        for i in range(dst.shape[0] // 128):
            line = jnp.broadcast_to(src[i * 128 : (i + 1) * 128][None], (128, 128))
            dst[i * 128 : (i + 1) * 128, :] = line.T

    @pl.when(south_later)
    def _():
        send_row(0, ready_south)

    await_winds(3)

    @pl.when(jnp.logical_not(last_band))
    def _():
        for half in range(2):
            halo_copy(1, half).wait_recv()

    advect(3, 0)
    finish(1)

    @pl.when(late_peer)
    def _():
        pl.semaphore_wait(ready_lev, 1)
        for p in range(2):
            flux_copy(p, count - lev).start()
            block_copy(p, count - lev).start()

    @pl.when(north_later)
    def _():
        send_row(1, ready_north)

    @pl.when(teller)
    def _():
        for off in ORDER:
            target = lax.rem(lev + off, count)
            pl.semaphore_signal(ring_count, 1, device_id={"lev": target}, device_id_type=MESH)
        pl.semaphore_wait(ring_count, count - 1)
        pl.semaphore_signal(ring_ready, 1, device_id={"lat": north}, device_id_type=MESH)

    for half in range(2):

        @pl.when(jnp.logical_not(first_band))
        def _():
            halo_copy(0, half).wait_recv()

        north_row(half)
        launch(2, (half,))

    def drain():
        @pl.when(has_south)
        def _():
            for half in range(2):
                halo_copy(0, half).wait_send()

        @pl.when(has_north)
        def _():
            for half in range(2):
                halo_copy(1, half).wait_send()

        for p in range(len(STAGES)):
            await_all(flux_out[p], flux_send_sem.at[p])
            await_all(send[p], send_sem.at[p])

    top = lax.broadcasted_iota(jnp.int32, (nlev, 128), 0) == 0

    def unpack(p):
        await_all(flux_in[p], flux_recv_sem.at[p])
        await_all(recv[p], recv_sem.at[p])
        recv[p][lev] = send[p][lev]
        flux_in[p][lev] = flux_out[p][lev]
        for i, r in enumerate(STAGES[p]):
            for pair in range(nfield // 2):
                pieces = ([], [])
                for g in range(16):
                    row = i * nfield * nlev + pair * 2 * nlev
                    both = recv[p][g, row : row + 2 * nlev].astype(jnp.float32)
                    for j in range(2):
                        piece = both[j * nlev : (j + 1) * nlev]
                        if g > 0:
                            k = i * nfield + 2 * pair + j
                            edge = flux_in[p][g - 1].astype(jnp.float32)[k : k + 1]
                            edge = jnp.broadcast_to(edge, (nlev, 128))
                            piece = piece + jnp.where(top, edge, 0.0)
                        pieces[j].append(piece)
                for j in range(2):
                    f = 2 * pair + j
                    whole = jnp.concatenate(pieces[j], axis=0)
                    ob[r, f * 128 : (f + 1) * 128] = whole
                    x_buf[f * 128 : (f + 1) * 128, i * 128 : (i + 1) * 128] = whole.astype(
                        jnp.bfloat16
                    )

    def physics(p):
        rows = STAGES[p]
        cols = 128 * len(rows)

        def wide(value):
            return jnp.concatenate([value] * len(rows), axis=1)

        x = x_buf[:, 0:cols]
        for start in range(0, 768, 256):
            span = slice(start, start + 256)
            v = jnp.dot(w1t[span], x, preferred_element_type=jnp.float32)
            h1[span, 0:cols] = silu(v + wide(b1[span])).astype(jnp.bfloat16)
        x = h1[:, 0:cols]
        for start in range(0, 640, 128):
            span = slice(start, start + 128)
            v = jnp.dot(w2t[span], x, preferred_element_type=jnp.float32)
            h2[span, 0:cols] = silu(v + wide(b2[span])).astype(jnp.bfloat16)
        x = h2[:, 0:cols]
        active = []
        for r in rows:
            hit = own_ref[0, 0, 0] == r
            for other in (own_ref[0, 0, 1], lent_ref[0, 0, 0], lent_ref[0, 0, 1]):
                hit = jnp.logical_or(hit, other == r)
            active.append(hit)
        for start in range(0, 512, 256):
            span = slice(start, start + 256)
            v = jnp.dot(w3t[span], x, preferred_element_type=jnp.float32)
            v = (v + wide(b3[span])).astype(jnp.bfloat16).astype(jnp.float32)
            for i, r in enumerate(rows):
                out[pl.ds(start * nrow + r, 256, stride=nrow), :] = ob[r, span] + jnp.where(
                    active[i], v[:, i * 128 : (i + 1) * 128], 0.0
                )

    for p in range(len(STAGES)):
        if p == len(STAGES) - 1:
            drain()
        unpack(p)
        physics(p)


ORDER = (8, 7, 9, 6, 10, 5, 11, 4, 12, 3, 13, 2, 14, 1, 15)


def in_hbm(value):
    return pltpu.with_memory_space_constraint(value, pltpu.HBM)


def body(
    fields,
    courant_lon,
    courant_lat,
    displacement,
    own_slot,
    lent_slot,
    w_first,
    bias_first,
    w_second,
    bias_second,
    w_third,
    bias_third,
):
    nfield, nlev, nrow, lon = fields.shape
    count = lax.axis_size("lev")
    width = nfield * nlev * count
    part = lon // count
    hidden = (w_first.shape[1], w_second.shape[1])
    f32, bf16 = jnp.float32, jnp.bfloat16
    hbm = pl.BlockSpec(memory_space=pltpu.HBM)
    dma = pltpu.SemaphoreType.DMA
    stages = len(STAGES)
    buffers = []
    for rows in STAGES:
        buffers += [pltpu.VMEM((count, len(rows) * nfield, part), bf16)] * 2
        buffers += [pltpu.VMEM((count, len(rows) * nfield * nlev, part), bf16)] * 2
    return pl.pallas_call(
        kernel,
        name="tracer",
        out_shape=jax.ShapeDtypeStruct((width * nrow, part), f32),
        in_specs=[hbm] * 12,
        out_specs=pl.BlockSpec(memory_space=pltpu.VMEM),
        scratch_shapes=[
            pltpu.VMEM((nfield, nrow, nlev, lon), f32),
            pltpu.VMEM((3, nrow, nlev, lon), f32),
            pltpu.VMEM((nfield, nrow, nlev, lon), f32),
            pltpu.VMEM((2, 2, nfield // 2, 2 * nlev, lon // 2), bf16),
            pltpu.VMEM((2, 2, nfield // 2, 2 * nlev, lon // 2), bf16),
            pltpu.VMEM((2 * nfield, lon), f32),
            *buffers,
            pltpu.VMEM((width, hidden[0]), bf16),
            pltpu.VMEM((hidden[0], hidden[1]), bf16),
            pltpu.VMEM((hidden[1], width), bf16),
            pltpu.VMEM((hidden[0], width), bf16),
            pltpu.VMEM((hidden[1], hidden[0]), bf16),
            pltpu.VMEM((width, hidden[1]), bf16),
            pltpu.VMEM((hidden[0], 128), f32),
            pltpu.VMEM((hidden[1], 128), f32),
            pltpu.VMEM((width, 128), f32),
            pltpu.VMEM((nrow, width, part), f32),
            pltpu.VMEM((width, 2 * part), bf16),
            pltpu.VMEM((hidden[0], 2 * part), bf16),
            pltpu.VMEM((hidden[1], 2 * part), bf16),
            pltpu.SMEM(own_slot.shape, jnp.int32),
            pltpu.SMEM(lent_slot.shape, jnp.int32),
            pltpu.VMEM(bias_first.shape, f32),
            pltpu.VMEM(bias_second.shape, f32),
            pltpu.VMEM(bias_third.shape, f32),
            dma((nrow,)),
            dma((nrow,)),
            dma((8,)),
            dma((2, 2)),
            dma((2, 2)),
            *[pltpu.SemaphoreType.REGULAR] * 5,
            dma((stages,)),
            dma((stages,)),
            dma((stages,)),
            dma((stages,)),
        ],
        compiler_params=pltpu.CompilerParams(
            collective_id=0, has_side_effects=True, vmem_limit_bytes=48 << 20
        ),
    )(
        in_hbm(fields),
        in_hbm(courant_lon),
        in_hbm(courant_lat),
        in_hbm(displacement),
        in_hbm(own_slot),
        in_hbm(lent_slot),
        in_hbm(w_first),
        in_hbm(bias_first),
        in_hbm(w_second),
        in_hbm(bias_second),
        in_hbm(w_third),
        in_hbm(bias_third),
    ).reshape(width, nrow, part)


def solution(mesh):
    in_specs = (
        P(None, "lev", "lat", None),
        P("lev", "lat", None),
        P("lev", "lat", None),
        P("lev", "lat", None),
        P("lev", "lat", None),
        P("lev", "lat", None),
        P(),
        P(),
        P(),
        P(),
        P(),
        P(),
    )
    out_specs = P(None, "lat", "lev")
    return jax.shard_map(body, mesh=mesh, in_specs=in_specs, out_specs=out_specs, check_vma=False)
```
